32 devices in a mesh: seq: 4 (over x, core), shard: 8 (over z, y).
Axes of the slice: x: 2, y: 2, z: 4, core: 2. Of those that a mesh axis runs over, the one named last changes fastest.
Arguments:
- inputs: bfloat16 [16, 2048, 768], P('shard', 'seq'), may hold values from -6 to 6
- first_gain: bfloat16 [768], P(('seq', 'shard')), may hold values from 0.25 to 1.75
- first_shift: bfloat16 [768], P(('seq', 'shard')), may hold values from -3 to 3
- second_gain: bfloat16 [768], P(('seq', 'shard')), may hold values from 0.25 to 1.75
- second_shift: bfloat16 [768], P(('seq', 'shard')), may hold values from -3 to 3
- packed_weight: bfloat16 [768, 2304], P(('seq', 'shard')), may hold values from -1.5 to 1.5
- packed_bias: bfloat16 [3, 768], P(None, ('seq', 'shard')), may hold values from -3 to 3
- output_weight: bfloat16 [768, 768], P(('seq', 'shard')), may hold values from -0.875 to 0.875
- output_bias: bfloat16 [768], P(('seq', 'shard')), may hold values from -3 to 3
- expand_weight: bfloat16 [768, 3072], P(('seq', 'shard')), may hold values from -0.21875 to 0.21875
- expand_bias: bfloat16 [3072], P(('seq', 'shard')), may hold values from -3 to 3
- reduce_weight: bfloat16 [3072, 768], P(('seq', 'shard')), may hold values from -0.109375 to 0.109375
- reduce_bias: bfloat16 [768], P(('seq', 'shard')), may hold values from -3 to 3
- cotangent: bfloat16 [16, 2048, 768], P('shard', 'seq'), may hold values from -6 to 6
Outputs:
- layer_out: bfloat16 [16, 2048, 768], P('shard', 'seq')
- input_grad: bfloat16 [16, 2048, 768], P('shard', 'seq')
- first_gain_grad: float32 [768], P(('seq', 'shard'))
- first_shift_grad: float32 [768], P(('seq', 'shard'))
- second_gain_grad: float32 [768], P(('seq', 'shard'))
- second_shift_grad: float32 [768], P(('seq', 'shard'))
- packed_weight_grad: float32 [768, 2304], P(('seq', 'shard'))
- packed_bias_grad: float32 [3, 768], P(None, ('seq', 'shard'))
- output_weight_grad: float32 [768, 768], P(('seq', 'shard'))
- output_bias_grad: float32 [768], P(('seq', 'shard'))
- expand_weight_grad: float32 [768, 3072], P(('seq', 'shard'))
- expand_bias_grad: float32 [3072], P(('seq', 'shard'))
- reduce_weight_grad: float32 [3072, 768], P(('seq', 'shard'))
- reduce_bias_grad: float32 [768], P(('seq', 'shard'))
The draws below stay inside these ranges and needn't reach their ends.
All inputs are finite; a program needn't handle non-finite values.
Results may differ from the reference program's by a relative error of at most 0.012.
Values may be sent and summed in bfloat16 or wider, within the bound.
No kernel may reach another device: no remote copies, remote signals or barrier semaphores. Data moves between devices by JAX's collectives and lax.ppermute only.
A program may use at most 448 MiB of HBM per device.

```python
import math
import jax
import jax.numpy as jnp
from jax import lax

D = 768
HEADS = 12
HD = 64
ROT = 16
FF = 3072
LENGTH = 2048
SEQS = 16


def draw_packed_weight(key, part):
    first_key = jax.random.fold_in(key, 11)
    base = jax.random.normal(first_key, (D, 3 * D), jnp.float32) * D ** (-0.5)
    return jnp.clip(base, -1.5, 1.5).astype(jnp.bfloat16)


def raised(entries, stream_key, source, target, shards_of, factor):
    def block_of(axis_at):
        return (jnp.arange(entries.shape[axis_at]) // (entries.shape[axis_at] // shards_of)).reshape((-1,) + (1,) * (entries.ndim - 1 - axis_at))

    one_side = jax.random.permutation(stream_key, shards_of)[block_of(target)]
    second = (block_of(target) + shards_of // 2) % shards_of
    return jnp.where((block_of(source) == one_side) | (block_of(source) == second), factor * entries, entries)


def level_of(rng, extent, shards, smallest, top_value):
    def one(dim, parts):
        heights = jax.random.uniform(jax.random.fold_in(jax.random.fold_in(rng, 6), dim), (parts,), jnp.float32, smallest / len(shards), top_value / len(shards))
        return jnp.repeat(jnp.exp(heights), extent[dim] // parts).reshape((-1,) + (1,) * (len(extent) - dim - 1))

    level = one(*shards[0])
    for cut in shards[1:]:
        level = level * one(*cut)
    return level


def centred(rng, dims, scale, bound, split=(), held_as=jnp.bfloat16):
    values = scale * jax.random.normal(rng, dims, jnp.float32)
    if split:
        values = values * level_of(rng, dims, split, -0.22, 0.18)
    return jnp.clip(values, -bound, bound).astype(held_as)


def bell_draw_with(rng, shape, scale, bound, cuts, heavy, kind=jnp.bfloat16):
    values = scale * jax.random.normal(rng, shape, jnp.float32)
    if cuts:
        values = values * level_of(rng, shape, cuts, -0.22, 0.18)
    return jnp.clip(raised(values, jax.random.fold_in(rng, 3), *heavy), -bound, bound).astype(kind)


def setup_inputs(seed: int = 0) -> dict:
    streams_of = jax.random.split(jax.random.key(seed), 15)
    inputs = centred(streams_of[0], (SEQS, LENGTH, D), 1.0, 6.0, ((0, 8), (1, 4)))
    first_gain = jnp.clip(1.0 + 0.15 * jax.random.normal(streams_of[1], (D,), jnp.float32), 0.25, 1.75).astype(jnp.bfloat16)
    first_shift = centred(streams_of[2], (D,), 0.5, 3.0, ((0, 32),))
    second_gain = jnp.clip(1.0 + 0.15 * jax.random.normal(streams_of[3], (D,), jnp.float32), 0.25, 1.75).astype(jnp.bfloat16)
    second_shift = centred(streams_of[4], (D,), 0.5, 3.0, ((0, 32),))
    packed_weight = draw_packed_weight(jax.random.fold_in(streams_of[14], 71), 0)
    packed_bias = centred(streams_of[6], (3, D), 0.5, 3.0, ((1, 32),))
    output_weight = centred(streams_of[7], (D, D), (D // 16) ** -0.5, 0.875, ((0, 32),))
    output_bias = centred(streams_of[8], (D,), 0.5, 3.0, ((0, 32),))
    expand_weight = centred(streams_of[9], (D, FF), D ** -0.5, 0.21875, ((0, 32),))
    expand_bias = centred(streams_of[10], (FF,), 0.5, 3.0, ((0, 32),))
    reduce_weight = centred(streams_of[11], (FF, D), FF ** -0.5, 0.109375, ((0, 32),))
    reduce_bias = centred(streams_of[12], (D,), 0.5, 3.0, ((0, 32),))
    cotangent = bell_draw_with(streams_of[13], (SEQS, LENGTH, D), 1.0, 6.0, ((0, 8), (1, 4)), (0, 2, 8, 2.0))
    return {"inputs": inputs, "first_gain": first_gain, "first_shift": first_shift, "second_gain": second_gain, "second_shift": second_shift, "packed_weight": packed_weight, "packed_bias": packed_bias, "output_weight": output_weight, "output_bias": output_bias, "expand_weight": expand_weight, "expand_bias": expand_bias, "reduce_weight": reduce_weight, "reduce_bias": reduce_bias, "cotangent": cotangent}


@jax.custom_vjp
def low(v):
    return lax.optimization_barrier(v.astype(jnp.bfloat16)).astype(jnp.float32)

@jax.custom_vjp
def low_back(v):
    return v

def low_keep(v):
    return (low(v), None)

def low_pass(kept, grad):
    return (grad,)

def back_keep(v):
    return (v, None)

def back_low(kept, grad):
    return (low(grad),)
low.defvjp(low_keep, low_pass)
low_back.defvjp(back_keep, back_low)
highest = lax.Precision.HIGHEST
eps_norm = 1e-05
rope_base = 10000.0
masked_score = -1e+30

def layer_norm(values, gain, shift):
    centre = values - lax.optimization_barrier(jnp.mean(values, axis=-1, keepdims=True))
    spread = lax.optimization_barrier(jnp.mean(centre * centre, axis=-1, keepdims=True))
    return centre * lax.rsqrt(spread + eps_norm) * gain + shift

def rotary_tables(positions):
    half_rot = ROT // 2
    frequency = rope_base ** (-(jnp.arange(half_rot, dtype=jnp.float32) * 2.0 / ROT))
    angles = positions[:, None] * frequency[None, :]
    return (jnp.cos(angles)[:, None, :], jnp.sin(angles)[:, None, :])

def rotate(heads, cosine, sine_table):
    half_rot = ROT // 2
    front = heads[..., :half_rot]
    behind = heads[..., half_rot:ROT]
    remain = heads[..., ROT:]
    return jnp.concatenate([front * cosine - behind * sine_table, behind * cosine + front * sine_table, remain], axis=-1)

def attention(queries, keyset, values):
    batch = queries.shape[0]
    block_rows = min(512, LENGTH)
    block_count = LENGTH // block_rows
    scaling = HD ** (-0.5)
    key_pos = jnp.arange(LENGTH, dtype=jnp.int32)

    def one_block(position):
        offset = (position * block_rows).astype(jnp.int32)
        query_rows = lax.dynamic_slice_in_dim(queries, offset, block_rows, 1)
        scores = jnp.einsum('bqhd,bkhd->bhqk', query_rows, keyset, precision=highest) * scaling
        scores = low_back(scores)
        query_pos = offset + jnp.arange(block_rows, dtype=jnp.int32)
        allowed = key_pos[None, :] <= query_pos[:, None]
        scores = jnp.where(allowed, scores, masked_score)
        largest = lax.optimization_barrier(jnp.max(scores, axis=-1, keepdims=True))
        weights = jnp.exp(scores - largest)
        probability = weights / lax.optimization_barrier(jnp.sum(weights, axis=-1, keepdims=True))
        return jnp.einsum('bhqk,bkhd->bqhd', low(probability), values, precision=highest)
    blocks = lax.map(jax.checkpoint(one_block), jnp.arange(block_count, dtype=jnp.int32))
    return jnp.moveaxis(blocks, 0, 1).reshape(batch, LENGTH, HEADS, HD)

def forward(inputs, params):
    first_gain, first_shift, second_gain, second_shift, packed_weight, packed_bias, output_weight, output_bias, expand_weight, expand_bias, reduce_weight, reduce_bias = params
    batch = inputs.shape[0]
    branch_one = low(layer_norm(inputs, first_gain, first_shift))
    branch_two = low(layer_norm(inputs, second_gain, second_shift))
    projected = jnp.einsum('btd,de->bte', branch_one, packed_weight, precision=highest) + packed_bias.reshape(3 * D)
    projected = low_back(projected).reshape(batch, LENGTH, 3, HEADS, HD)
    positions = jnp.arange(LENGTH, dtype=jnp.float32)
    cosine, sine_table = rotary_tables(positions)
    queries = low_back(low(rotate(projected[:, :, 0], cosine, sine_table)))
    keyset = low_back(low(rotate(projected[:, :, 1], cosine, sine_table)))
    values = low_back(low(projected[:, :, 2]))
    attended = attention(queries, keyset, values)
    attended = low_back(low(attended)).reshape(batch, LENGTH, D)
    attn_out = jnp.einsum('btd,de->bte', attended, output_weight, precision=highest) + output_bias
    hidden = low_back(jnp.einsum('btd,df->btf', branch_two, expand_weight, precision=highest) + expand_bias)
    active = low(jax.nn.gelu(hidden, approximate=False))
    mlp_out = jnp.einsum('btf,fd->btd', active, reduce_weight, precision=highest) + reduce_bias
    return inputs + attn_out + mlp_out

def reference(inputs, first_gain, first_shift, second_gain, second_shift, packed_weight, packed_bias, output_weight, output_bias, expand_weight, expand_bias, reduce_weight, reduce_bias, cotangent):
    params = tuple((element.astype(jnp.float32) for element in (first_gain, first_shift, second_gain, second_shift, packed_weight, packed_bias, output_weight, output_bias, expand_weight, expand_bias, reduce_weight, reduce_bias)))
    group_size = math.gcd(SEQS, max(1, 4096 // LENGTH))
    step_count = SEQS // group_size
    stacked_in = inputs.astype(jnp.float32).reshape(step_count, group_size, LENGTH, D)
    stacked_grad = cotangent.astype(jnp.float32).reshape(step_count, group_size, LENGTH, D)

    def one_step(totals, pair):
        stretch_in, stretch_grad = pair
        result, pullback = jax.vjp(forward, stretch_in, params)
        input_part, param_part = pullback(stretch_grad)
        totals = jax.tree.map(jnp.add, totals, param_part)
        return (totals, (result.astype(jnp.bfloat16), input_part.astype(jnp.bfloat16)))
    zeros = tuple((jnp.zeros_like(element) for element in params))
    totals, (results, input_grads) = lax.scan(one_step, zeros, (stacked_in, stacked_grad))
    results = results.reshape(SEQS, LENGTH, D)
    input_grads = input_grads.reshape(SEQS, LENGTH, D)
    return (results, input_grads, totals[0], totals[1], totals[2], totals[3], totals[4], totals[5], totals[6], totals[7], totals[8], totals[9], totals[10], totals[11])
```

```python
import functools
import jax, jax.numpy as jnp
from jax import lax
from jax.experimental import pallas as pl
from jax.experimental.pallas import tpu as pltpu
from jax.sharding import Mesh, PartitionSpec as P

HD=64
ROT=16
f32=jnp.float32; bf16=jnp.bfloat16

def dot(a,b): return jnp.dot(a,b,preferred_element_type=f32)

def turn(v,tab,back):
    sgn=-1.0 if back else 1.0
    return v*tab[0]+sgn*(pltpu.roll(v,120,1)*tab[1]+pltpu.roll(v,8,1)*tab[2])

def attn_body(c_ref, own, par, tab, keep, send, qs, ks, gs, vs, qT, gT, kT, vT, es, oT, dqT, dk, dv, *, blk, length):
    c=c_ref[0]
    half=blk
    nb=length//blk
    lane=lax.broadcasted_iota(jnp.int32,(1,128),1)
    first=lane<HD
    for j,(d,dT) in enumerate(((qs,qT),(ks,kT),(vs,vT),(gs,gT))):
        for h in range(nb//2):
            a=own[j,h*blk:(h+1)*blk,:]; b=par[j,h*blk:(h+1)*blk,:]
            pa=pl.multiple_of((2*h+c)*blk,blk); pb=pl.multiple_of((2*h+1-c)*blk,blk)
            d[pl.ds(pa,blk),:]=a
            d[pl.ds(pb,blk),:]=b
            dT[2*h+c]=a.T
            dT[2*h+1-c]=b.T
    dk[...]=jnp.zeros_like(dk); dv[...]=jnp.zeros_like(dv)
    kk=HD**-0.5*1.4426950408889634
    rowi=lax.broadcasted_iota(jnp.int32,(blk,blk),0)
    coli=lax.broadcasted_iota(jnp.int32,(blk,blk),1)
    allowed=rowi<=coli
    zero64=jnp.zeros((HD,blk),bf16)

    def block(i,_):
        qt=qT[i]; gt=gT[i]
        qh=[jnp.concatenate([qt[:HD],zero64],0),jnp.concatenate([zero64,qt[HD:]],0)]
        gh=[jnp.concatenate([gt[:HD],zero64],0),jnp.concatenate([zero64,gt[HD:]],0)]
        rows=pl.ds(pl.multiple_of(i*blk,blk),blk)
        q=qs[rows,:]; g=gs[rows,:]
        zq=jnp.zeros_like(q)
        qm=[jnp.where(first,q,zq),jnp.where(first,zq,q)]
        gm=[jnp.where(first,g,zq),jnp.where(first,zq,g)]
        def fold(x,op):
            return functools.reduce(op,[x[r*8:(r+1)*8] for r in range(blk//8)])
        def sA(j,m):
            kr=pl.ds(pl.multiple_of(j*blk,blk),blk)
            k=ks[kr,:]
            out=[]
            for h in range(2):
                s=dot(k,qh[h])
                es[h,kr,:]=s
                out.append(jnp.maximum(m[h],jnp.max(s.reshape(blk//8,8,blk),axis=0)))
            return tuple(out)
        m0=jnp.full((8,blk),-1e30,f32)
        k=ks[rows,:]
        m=[]
        for h in range(2):
            s=jnp.where(allowed,dot(k,qh[h]),-1e30)
            es[h,rows,:]=s
            m.append(jnp.max(s.reshape(blk//8,8,blk),axis=0))
        m=lax.fori_loop(0,i,sA,tuple(m))
        mk=[jnp.max(t,axis=0,keepdims=True)*kk for t in m]
        oT[...]=jnp.zeros_like(oT)
        def sB(j,l):
            kr=pl.ds(pl.multiple_of(j*blk,blk),blk)
            out=[]
            for h in range(2):
                e=jnp.exp2(es[h,kr,:]*kk-mk[h])
                es[h,kr,:]=e
                out.append(l[h]+jnp.sum(e.reshape(blk//8,8,blk),axis=0))
                oT[h*HD:(h+1)*HD,:]+=dot(vT[j,h*HD:(h+1)*HD,:],e.astype(bf16))
            return tuple(out)
        z=jnp.zeros((8,blk),f32)
        l=lax.fori_loop(0,i+1,sB,(z,z))
        r=[1.0/jnp.sum(t,axis=0,keepdims=True) for t in l]
        o=[oT[h*HD:(h+1)*HD,:]*r[h] for h in range(2)]
        D=[jnp.sum(o[h]*gt[h*HD:(h+1)*HD].astype(f32),axis=0,keepdims=True) for h in range(2)]
        oT[...]=jnp.concatenate(o,0)
        dqT[...]=jnp.zeros_like(dqT)
        def sC(j,_):
            kr=pl.ds(pl.multiple_of(j*blk,blk),blk)
            v=vs[kr,:]
            pb=[];db=[]
            for h in range(2):
                p=es[h,kr,:]*r[h]
                ds=(p*(dot(v,gh[h])-D[h])).astype(bf16)
                pb.append(p.astype(bf16)); db.append(ds)
                dqT[h*HD:(h+1)*HD,:]+=dot(kT[j,h*HD:(h+1)*HD,:],ds)
            dv[kr,:]+=dot(pb[0],gm[0])+dot(pb[1],gm[1])
            dk[kr,:]+=dot(db[0],qm[0])+dot(db[1],qm[1])
            return 0
        lax.fori_loop(0,i+1,sC,0)
        qs[rows,:]=(dqT[...].T*HD**-0.5).astype(bf16)
        gs[rows,:]=oT[...].T.astype(bf16)
        return 0
    lax.fori_loop(0,nb,block,0)
    for h in range(nb//2):
        for who,ref in ((c,keep),(1-c,send)):
            rows=pl.ds(pl.multiple_of((2*h+who)*blk,blk),blk)
            dst=slice(h*blk,(h+1)*blk)
            t=[tab[n,rows,:] for n in range(3)]
            ref[0,dst,:]=gs[rows,:]
            ref[1,dst,:]=turn(qs[rows,:].astype(f32),t,True).astype(bf16)
            ref[2,dst,:]=turn((dk[rows,:]*HD**-0.5).astype(bf16).astype(f32),t,True).astype(bf16)
            ref[3,dst,:]=dv[rows,:].astype(bf16)

def attention(c, own, par, tab, pair, npair=1, blk=512):
    rows=own.shape[1]; length=2*rows
    nb=length//blk
    spec=pl.BlockSpec((4,rows,128),lambda p,c:(0,0,p+pair))
    ospec=pl.BlockSpec((4,rows,128),lambda p,c:(0,0,p))
    V=pltpu.VMEM
    return pl.pallas_call(
        functools.partial(attn_body,blk=blk,length=length),
        out_shape=(jax.ShapeDtypeStruct((4,rows,128*npair),bf16),)*2,
        grid_spec=pltpu.PrefetchScalarGridSpec(num_scalar_prefetch=1,grid=(npair,),
            in_specs=[spec,spec,pl.BlockSpec((3,length,128),lambda p,c:(0,0,0),pipeline_mode=pl.Buffered(1))],
            out_specs=[ospec,ospec],
            scratch_shapes=[V((length,128),bf16)]*4+[V((nb,128,blk),bf16)]*4+
              [V((2,length,blk),f32),V((128,blk),f32),V((128,blk),f32),V((length,128),f32),V((length,128),f32)]),
        compiler_params=pltpu.CompilerParams(vmem_limit_bytes=56<<20),
        name="attention",
        cost_estimate=pl.CostEstimate(flops=int(6*2*length*length//2*HD*2*npair*4),transcendentals=length*length*npair,bytes_accessed=16*rows*128*2*npair),
    )(c,own,par,tab)
eps_norm = 1e-05
rope_base = 10000.0

def dot_nt(a,b): return lax.dot_general(a,b,(((1,),(1,)),((),())),preferred_element_type=f32)
def dot_tn(a,b): return lax.dot_general(a,b,(((0,),(0,)),((),())),preferred_element_type=f32)

def norm_of(x):
    x=x.astype(f32)
    ce=x-jnp.mean(x,axis=-1,keepdims=True)
    inv=lax.rsqrt(jnp.mean(ce*ce,axis=-1,keepdims=True)+eps_norm)
    return ce*inv,inv

def norm_back(up,normed,inv,gain):
    s=up*gain
    return inv*(s-jnp.mean(s,axis=-1,keepdims=True)-normed*jnp.mean(s*normed,axis=-1,keepdims=True))

WHOLE=lambda shape: pl.BlockSpec(shape,lambda *a:(0,)*len(shape),pipeline_mode=pl.Buffered(1))

def quarter(me_ref,n):
    return (me_ref[0]^(n//2))*2+(me_ref[1]^(n%2))

def proj_body(me, t, u, w0,w1,w2,w3, o0,o1,o2,o3, bias, gain, shift, tab, out, ws, wos, *, group):
    gc=me[1]^group
    @pl.when(pl.program_id(0)==0)
    def _():
        q=w0.shape[0]
        for n,(w,o) in enumerate(((w0,o0),(w1,o1),(w2,o2),(w3,o3))):
            rows=pl.ds(pl.multiple_of(quarter(me,n)*q,q),q)
            for j in range(6): ws[j,rows,:]=w[:,j*384:(j+1)*384]
            wos[rows,:]=o[...]
    normed,_=norm_of(t[...])
    b1=(normed*gain[...]+shift[...]).astype(bf16)
    for j in range(3):
        v=dot(b1,ws[2*j+gc])+bias[0,j:j+1,:]
        if j<2:
            tb=[tab[n] for n in range(3)]
            v=jnp.concatenate([turn(v[:,a*128:(a+1)*128],tb,False) for a in range(3)],1)
        out[j]=v.astype(bf16)
    out[3]=dot_nt(u[...],wos[pl.ds(pl.multiple_of(gc*384,384),384),:]).astype(bf16)

def project(me,t,u,wq,oq,bias,gain,shift,tab,group,rb=256):
    n=t.shape[0]; per=n//2//rb
    rs=pl.BlockSpec((rb,768),lambda i,me:(i,0))
    return pl.pallas_call(functools.partial(proj_body,group=group),
        out_shape=jax.ShapeDtypeStruct((4,n,384),bf16),
        grid_spec=pltpu.PrefetchScalarGridSpec(num_scalar_prefetch=1,grid=(n//rb,),
            in_specs=[rs,rs]+[WHOLE(w.shape) for w in wq]+[WHOLE(w.shape) for w in oq]+
              [pl.BlockSpec((1,3,384),lambda i,me:(me[1]^group,0,0)),WHOLE((1,768)),WHOLE((1,768)),
               pl.BlockSpec((3,rb,128),lambda i,me:(0,(2*(i//per)+me[1])*per+i%per,0))],
            out_specs=pl.BlockSpec((4,rb,384),lambda i,me:(0,i,0)),
            scratch_shapes=[pltpu.VMEM((6,768,384),bf16),pltpu.VMEM((768,768),bf16)]),
        compiler_params=pltpu.CompilerParams(vmem_limit_bytes=56<<20),
        name="project",
        cost_estimate=pl.CostEstimate(flops=2*n*768*1536*2,transcendentals=n,bytes_accessed=n*768*4+768*3072*2+n*1536*2),
    )(me,t,u,*wq,*oq,bias,gain,shift,tab)

def back_body(me, ka, ra, u, t, w0,w1,w2,w3, o0,o1,o2,o3, obias, gain, shift,
              base, og, pg, acc1, sums, pbs, ws, wos, b1T, acc, gs):
    s=pl.program_id(0)
    c=me[1]
    @pl.when(s==0)
    def _():
        q=w0.shape[0]
        for n,(w,o) in enumerate(((w0,o0),(w1,o1),(w2,o2),(w3,o3))):
            rows=pl.ds(pl.multiple_of(quarter(me,n)*q,q),q)
            for j in range(6): ws[j,rows,:]=w[:,j*384:(j+1)*384]
            wos[rows,:]=o[...]
        acc[...]=t[...].astype(f32)+obias[...]
        sums[...]=jnp.zeros_like(sums)
        sums[2:3,:]=jnp.sum(u[...].astype(f32),axis=0,keepdims=True)
        normed,_=norm_of(t[...])
        b1T[...]=(normed*gain[...]+shift[...]).astype(bf16).T
    for g,a in ((0,ka),(1,ra)):
        gc=c^g
        @pl.when(s==g)
        def _():
            rows=pl.ds(pl.multiple_of(gc*384,384),384)
            acc[...]+=dot(a[0],wos[rows,:])
            gs[rows,:]=dot_tn(a[0],u[...])
            if g==1:
                base[...]=acc[...]
                for n in range(4):
                    og[n]=gs[pl.ds(pl.multiple_of(quarter(me,n)*192,192),192),:].astype(bf16)
                acc[...]=jnp.zeros_like(acc)
    @pl.when(s>=2)
    def _():
        use_mine=s<5
        j=jnp.where(use_mine,s-2,s-5)
        gc=jnp.where(use_mine,c,1-c)
        def one(a):
            p=a[0]
            acc[...]+=dot_nt(p,ws[2*j+gc])
            gs[:,:384]=dot(b1T[...],p)
            pbs[0]=jnp.sum(p.astype(f32),axis=0,keepdims=True)
        @pl.when(use_mine)
        def _(): one(ka)
        @pl.when(jnp.logical_not(use_mine))
        def _(): one(ra)
        for n in range(4):
            pg[n]=gs[pl.ds(pl.multiple_of(quarter(me,n)*192,192),192),:384].astype(bf16)
    @pl.when(s==7)
    def _():
        normed,inv=norm_of(t[...])
        b=acc[...]
        sums[0:1,:]=jnp.sum(b*normed,axis=0,keepdims=True)
        sums[1:2,:]=jnp.sum(b,axis=0,keepdims=True)
        acc1[...]=u[...].astype(f32)+norm_back(b,normed,inv,gain[...])

def back(me,keep,recv,u,t,wq,oq,obias,gain,shift):
    n=t.shape[0]
    def kmap(s,me): return (jnp.where(s<2,0,jnp.clip(s-1,1,3)),0,0)
    def rmap(s,me): return (jnp.where(s<5,0,s-4),0,0)
    def col(s,me):
        j=jnp.where(s<5,jnp.maximum(s-2,0),s-5); gc=jnp.where(s<5,me[1],1-me[1])
        return 2*j+gc
    return pl.pallas_call(back_body,
        out_shape=(jax.ShapeDtypeStruct((n,768),f32),jax.ShapeDtypeStruct((4,192,768),bf16),
                   jax.ShapeDtypeStruct((4,192,2304),bf16),jax.ShapeDtypeStruct((n,768),f32),
                   jax.ShapeDtypeStruct((8,768),f32),jax.ShapeDtypeStruct((6,1,384),f32)),
        grid_spec=pltpu.PrefetchScalarGridSpec(num_scalar_prefetch=1,grid=(8,),
            in_specs=[pl.BlockSpec((1,n,384),kmap),pl.BlockSpec((1,n,384),rmap),WHOLE((n,768)),WHOLE((n,768))]+
              [WHOLE(w.shape) for w in wq]+[WHOLE(w.shape) for w in oq]+[WHOLE((1,768))]*3,
            out_specs=[WHOLE((n,768)),WHOLE((4,192,768)),pl.BlockSpec((4,192,384),lambda s,me:(0,0,col(s,me))),
                       WHOLE((n,768)),WHOLE((8,768)),pl.BlockSpec((1,1,384),lambda s,me:(col(s,me),0,0))],
            scratch_shapes=[pltpu.VMEM((6,768,384),bf16),pltpu.VMEM((768,768),bf16),pltpu.VMEM((768,n),bf16),
                            pltpu.VMEM((n,768),f32),pltpu.VMEM((768,768),f32)]),
        compiler_params=pltpu.CompilerParams(vmem_limit_bytes=58<<20),
        name="back",
        cost_estimate=pl.CostEstimate(flops=2*n*768*768*8,transcendentals=n,bytes_accessed=n*768*24+768*3072*6),
    )(me,keep,recv,u,t,*wq,*oq,obias,gain,shift)

def mlp_body(*refs, last):
    (me,t,u,e0,e1,e2,e3,r0,r1,r2,r3,be,gain,shift)=refs[:14]
    refs=refs[14:]
    if last: (pm,pb,base,acc1),refs=refs[:4],refs[4:]
    rg,eg,eb=refs[:3]; refs=refs[3:]
    if last: (lo,ig,sums),refs=refs[:3],refs[3:]
    else: (om,ob),refs=refs[:2],refs[2:]
    b2,b2T,we,wr,act,hg,am,ab,egs=refs
    s=pl.program_id(0)
    n=t.shape[0]; rb=256
    @pl.when(s==0)
    def _():
        for i,r in enumerate((r0,r1,r2,r3)): wr[i]=r[...]
        def one(i,_):
            rows=pl.ds(pl.multiple_of(i*rb,rb),rb)
            normed,_=norm_of(t[rows,:])
            b=(normed*gain[...]+shift[...]).astype(bf16)
            b2[rows,:]=b
            b2T[i]=b.T
            if last:
                am[rows,:]=pm[rows,:]; ab[rows,:]=pb[rows,:]
            else:
                am[rows,:]=jnp.zeros((rb,768),f32); ab[rows,:]=jnp.zeros((rb,768),f32)
            return 0
        lax.fori_loop(0,n//rb,one,0)
    for i,e in enumerate((e0,e1,e2,e3)):
        we[pl.ds(pl.multiple_of(quarter(me,i)*192,192),192),:]=e[...]
    w_e=we[...]; w_r=wr[s]
    fb=384
    def one(i,bs):
        rows=pl.ds(pl.multiple_of(i*rb,rb),rb)
        h=dot(b2[rows,:],w_e)+be[0]
        ag=dot_nt(u[rows,:],w_r)
        cdf=0.5+0.5*lax.erf(h*0.7071067811865476)
        a=(h*cdf).astype(bf16)
        d=(ag*(cdf+h*(0.3989422804014327*jnp.exp(h*h*-0.5)))).astype(bf16)
        act[rows,:]=a; hg[rows,:]=d
        am[rows,:]+=dot(a,w_r)
        ab[rows,:]+=dot_nt(d,w_e)
        return bs+jnp.sum(d.astype(f32).reshape(rb//8,8,fb),axis=0)
    bs=lax.fori_loop(0,n//rb,one,jnp.zeros((8,fb),f32))
    eb[0]=jnp.sum(bs,axis=0,keepdims=True)
    rg[0]=dot_tn(act[...],u[...]).astype(bf16)
    x=jnp.zeros((768,fb),f32)
    for i in range(n//rb): x=x+dot(b2T[i],hg[i*rb:(i+1)*rb,:])
    egs[...]=x
    for i in range(4):
        eg[i]=egs[pl.ds(pl.multiple_of(quarter(me,i)*192,192),192),:].astype(bf16)
    @pl.when(s==3)
    def _():
        if last:
            def fin(i,c):
                rows=pl.ds(pl.multiple_of(i*rb,rb),rb)
                lo[rows,:]=(base[rows,:]+am[rows,:]).astype(bf16)
                normed,inv=norm_of(t[rows,:])
                b=ab[rows,:]
                ig[rows,:]=(acc1[rows,:]+norm_back(b,normed,inv,gain[...])).astype(bf16)
                return c[0]+jnp.sum(b*normed,axis=0,keepdims=True),c[1]+jnp.sum(b,axis=0,keepdims=True)
            z=jnp.zeros((1,768),f32)
            p,q=lax.fori_loop(0,n//rb,fin,(z,z))
            sums[...]=jnp.zeros_like(sums)
            sums[0:1,:]=p; sums[1:2,:]=q
        else:
            om[...]=am[...]; ob[...]=ab[...]

def mlp(me,t,u,eq,rq,be,gain,shift,k,extra=None):
    n=t.shape[0]; last=extra is not None
    def qa(s,me): return (me[0]^(s//2))*2+(me[1]^(s%2))
    S=jax.ShapeDtypeStruct; V=pltpu.VMEM
    acc=[S((n,768),f32)]*2
    return pl.pallas_call(functools.partial(mlp_body,last=last),
        out_shape=[S((4,384,768),bf16),S((4,192,1536),bf16),S((4,1,384),f32)]+
          ([S((n,768),bf16)]*2+[S((8,768),f32)] if last else acc),
        grid_spec=pltpu.PrefetchScalarGridSpec(num_scalar_prefetch=1,grid=(4,),
            in_specs=[WHOLE((n,768))]*2+[pl.BlockSpec((192,384),lambda s,me:(0,2*qa(s,me)+k))]*4+
              [pl.BlockSpec((384,768),lambda s,me:(k,0),pipeline_mode=pl.Buffered(1))]*4+
              [pl.BlockSpec((1,1,384),lambda s,me:(2*qa(s,me)+k,0,0))]+[WHOLE((1,768))]*2+
              ([WHOLE((n,768))]*4 if last else []),
            out_specs=[pl.BlockSpec((1,384,768),lambda s,me:(s,0,0)),pl.BlockSpec((4,192,384),lambda s,me:(0,0,qa(s,me))),
                       pl.BlockSpec((1,1,384),lambda s,me:(qa(s,me),0,0))]+[WHOLE((n,768))]*2+([WHOLE((8,768))] if last else []),
            scratch_shapes=[V((n,768),bf16),V((n//256,768,256),bf16),V((768,384),bf16),V((4,384,768),bf16),V((n,384),bf16),V((n,384),bf16),
                            V((n,768),f32),V((n,768),f32),V((768,384),f32)]),
        compiler_params=pltpu.CompilerParams(vmem_limit_bytes=60<<20),
        name="feed",
        cost_estimate=pl.CostEstimate(flops=6*2*n*768*1536,transcendentals=n*1536*2,bytes_accessed=n*768*20+768*1536*8),
    )(me,t,u,*eq,*rq,be,gain,shift,*(extra or ()))

def swap(a, axis):
    return lax.ppermute(a, axis, [(0, 1), (1, 0)])


def shift(a, axis, size, step):
    return lax.ppermute(a, axis, [(i, (i + step) % size) for i in range(size)])


def pick(index, here, there):
    place = lax.broadcasted_iota(jnp.int32, (2,) + (1,) * here.ndim, 0)
    return jnp.where(place == index, here[None], there[None])


def gather_line(shard, m):
    z = lax.axis_index("z")
    line = jnp.zeros((m,) + shard.shape, shard.dtype)
    line = lax.dynamic_update_index_in_dim(line, shard, z, 0)
    for step in range(1, m):
        line = lax.dynamic_update_index_in_dim(line, shift(shard, "z", m, step), (z - step) % m, 0)
    return line


def gather_quarters(shard, m, x_first):
    y = lax.axis_index("y")
    line = gather_line(shard, m)
    flat = (-1,) + shard.shape[1:]

    def join(a, b):
        return jnp.moveaxis(pick(y, a, b), 0, 1).reshape(flat)

    if x_first:
        far = swap(line, "x")
        near = join(line, swap(line, "y"))
        far = join(far, swap(far, "y"))
    else:
        near = join(line, swap(line, "y"))
        far = swap(near, "x")
    return [near, swap(near, "c"), far, swap(far, "c")]


def add(a, b, dtype):
    return (a.astype(f32) + b.astype(f32)).astype(dtype)


def scatter_plane(quarters, parts, x_first):
    y = lax.axis_index("y")
    near = add(quarters[0], swap(quarters[1], "c"), bf16)
    far = add(quarters[2], swap(quarters[3], "c"), bf16)

    def halve(a, dtype):
        a = a.reshape((parts, 2, -1) + a.shape[1:])
        keep = lax.dynamic_index_in_dim(a, y, 1, keepdims=False)
        send = lax.dynamic_index_in_dim(a, 1 - y, 1, keepdims=False)
        return add(keep, swap(send, "y"), dtype)

    if x_first:
        return halve(add(near, swap(far, "x"), bf16), bf16)
    near, far = halve(near, bf16), halve(far, bf16)
    return add(near, swap(far, "x"), bf16)


def scatter_line(line, m):
    z = lax.axis_index("z")
    total = lax.dynamic_index_in_dim(line, z, 0, keepdims=False).astype(f32)
    for step in range(1, m):
        part = lax.dynamic_index_in_dim(line, (z + step) % m, 0, keepdims=False)
        total = total + shift(part, "z", m, step).astype(f32)
    return total


def scatter_small(values, m):
    x, c, z, y = (lax.axis_index(a) for a in "xczy")
    values = values.reshape((2, 2, m, 2, -1))

    def halve(a, axis, index, name):
        keep = lax.dynamic_index_in_dim(a, index, axis, keepdims=False)
        send = lax.dynamic_index_in_dim(a, 1 - index, axis, keepdims=False)
        return keep + swap(send, name)

    values = halve(values, 1, c, "c")
    values = halve(values, 0, x, "x")
    values = halve(values, 1, y, "y")
    return scatter_line(values, m)


def rotary(length):
    half = ROT // 2
    frequency = rope_base ** (-(jnp.arange(half, dtype=f32) * 2.0 / ROT))
    angles = jnp.arange(length, dtype=jnp.int32).astype(f32)[:, None] * frequency[None, :]
    co, si = jnp.cos(angles), jnp.sin(angles)
    rest = jnp.zeros((length, HD - ROT), f32)
    none = jnp.zeros((length, half), f32)
    tables = (
        jnp.concatenate([co, co, rest + 1.0], 1),
        jnp.concatenate([-si, none, rest], 1),
        jnp.concatenate([none, si, rest], 1),
    )
    return jnp.stack([jnp.tile(t, (1, 2)) for t in tables])


def exchange(mine, x):
    other = swap(lax.dynamic_index_in_dim(mine, 1 - x, 0, keepdims=False), "x")
    place = lax.broadcasted_iota(jnp.int32, (2, 1, 1), 0)
    return jnp.where(place == x, mine, other[None])


def shards(
    inputs,
    first_gain,
    first_shift,
    second_gain,
    second_shift,
    packed_weight,
    packed_bias,
    output_weight,
    output_bias,
    expand_weight,
    expand_bias,
    reduce_weight,
    reduce_bias,
    cotangent,
    *,
    m,
):
    x, c = lax.axis_index("x"), lax.axis_index("c")
    me = jnp.stack([x, c]).astype(jnp.int32)
    width = inputs.shape[-1]
    block = inputs.shape[1]
    count = 4 * m * 2
    r = first_gain.shape[0]

    vectors = jnp.concatenate(
        [first_gain, first_shift, second_gain, second_shift, output_bias, reduce_bias]
        + [packed_bias[j] for j in range(3)]
        + [expand_bias]
    )
    small = gather_quarters(vectors[None, :], m, True)
    packed_q = gather_quarters(packed_weight, m, True)
    output_q = gather_quarters(output_weight, m, False)
    expand_q = gather_quarters(expand_weight, m, True)
    reduce_q = gather_quarters(reduce_weight, m, False)

    near = pick(c, small[0], small[1])
    far = pick(c, small[2], small[3])
    whole = pick(x, near, far).reshape(count, -1).astype(f32)
    rows = whole[:, : 9 * r].reshape(count, 9, r).transpose(1, 0, 2).reshape(9, width)
    gain_one, shift_one, gain_two, shift_two = (rows[i : i + 1] for i in range(4))
    out_add = rows[4:5] + rows[5:6]
    packed_add = rows[6:9].reshape(3, 2, width // 2).transpose(1, 0, 2)
    expand_add = whole[:, 9 * r :].reshape(-1, 1, 384)

    t = exchange(inputs, x).reshape(-1, width)
    u = exchange(cotangent, x).reshape(-1, width)
    table = rotary(4 * block)

    send = project(me, t, u, packed_q, output_q, packed_add, gain_one, shift_one, table, 1)
    own = project(me, t, u, packed_q, output_q, packed_add, gain_one, shift_one, table, 0)
    keep, give = attention(me[1:], own, swap(send, "c"), table, 0, npair=3)
    base, og, pg, first, sums_one, pb = back(
        me, keep, swap(give, "c"), u, t, packed_q, output_q, out_add, gain_one, shift_one
    )
    rg0, eg0, eb0, mid, low = mlp(me, t, u, expand_q, reduce_q, expand_add, gain_two, shift_two, 0)
    rg1, eg1, eb1, layer_out, input_grad, sums_two = mlp(
        me, t, u, expand_q, reduce_q, expand_add, gain_two, shift_two, 1, (mid, low, base, first)
    )
    layer_out = exchange(layer_out.reshape(inputs.shape), x)
    input_grad = exchange(input_grad.reshape(inputs.shape), x)

    packed_grad = scatter_line(scatter_plane(list(pg), m, True), m)
    output_grad = scatter_line(scatter_plane(list(og), m, False), m)
    reduce_grad = scatter_line(
        jnp.concatenate(
            [scatter_plane(list(rg0), m // 2, False), scatter_plane(list(rg1), m // 2, False)], 0
        ),
        m,
    )
    expand_grad = jnp.stack(
        [
            scatter_line(scatter_plane(list(e), m, True), m).reshape(r, 4, 384) for e in (eg0, eg1)
        ],
        axis=2,
    ).reshape(r, -1)

    vecs = jnp.concatenate([sums_one[:3], sums_two[:2], pb.reshape(3, width)], 0)
    vecs = vecs.reshape(8, count, r).transpose(1, 0, 2).reshape(count, 8 * r)
    ebs = jnp.stack([eb0, eb1], 1).reshape(count, -1)
    tiny = scatter_small(jnp.concatenate([vecs, ebs], 1), m)
    v = tiny[: 8 * r].reshape(8, r)
    return (
        layer_out,
        input_grad,
        v[0],
        v[1],
        v[3],
        v[4],
        packed_grad,
        v[5:8],
        output_grad,
        v[2],
        expand_grad,
        tiny[8 * r :],
        reduce_grad,
        v[2],
    )


def solution(mesh):
    shard = mesh.shape["shard"]
    m = shard // 2
    fine = Mesh(mesh.devices.reshape(2, 2, m, 2), ("x", "c", "z", "y"))
    every = ("x", "c", "z", "y")
    tokens = P(("z", "y"), ("x", "c"), None)
    vec, mat = P(every), P(every, None)
    in_specs = (tokens, vec, vec, vec, vec, mat, P(None, every), mat, vec, mat, vec, mat, vec, tokens)
    out_specs = (tokens, tokens, vec, vec, vec, vec, mat, P(None, every), mat, vec, mat, vec, mat, vec)
    return jax.shard_map(
        functools.partial(shards, m=m), mesh=fine, in_specs=in_specs, out_specs=out_specs, check_vma=False
    )
```

```python
import functools
import jax, jax.numpy as jnp
from jax import lax
from jax.experimental import pallas as pl
from jax.experimental.pallas import tpu as pltpu
from jax.sharding import Mesh, PartitionSpec as P

HD=64
ROT=16
f32=jnp.float32; bf16=jnp.bfloat16

def dot(a,b): return jnp.dot(a,b,preferred_element_type=f32)

def turn(v,tab,back):
    sgn=-1.0 if back else 1.0
    return v*tab[0]+sgn*(pltpu.roll(v,120,1)*tab[1]+pltpu.roll(v,8,1)*tab[2])

def attn_body(c_ref, own, par, gown, gpar, tab, keep, send, qs, ks, gs, vs, qT, gT, kT, vT, es, oT, dqT, dk, dv, *, blk, length):
    c=c_ref[0]
    nb=length//blk
    lane=lax.broadcasted_iota(jnp.int32,(1,128),1)
    first=lane<HD
    for j,(d,dT) in enumerate(((qs,qT),(ks,kT),(vs,vT),(gs,gT))):
        for h in range(nb//2):
            hr=slice(h*blk,(h+1)*blk)
            a,b=(own[j,hr,:],par[j,hr,:]) if j<3 else (gown[hr,:],gpar[hr,:])
            pa=pl.multiple_of((2*h+c)*blk,blk); pb=pl.multiple_of((2*h+1-c)*blk,blk)
            d[pl.ds(pa,blk),:]=a
            d[pl.ds(pb,blk),:]=b
            dT[2*h+c]=a.T
            dT[2*h+1-c]=b.T
    dk[...]=jnp.zeros_like(dk); dv[...]=jnp.zeros_like(dv)
    kk=HD**-0.5*1.4426950408889634
    rowi=lax.broadcasted_iota(jnp.int32,(blk,blk),0)
    coli=lax.broadcasted_iota(jnp.int32,(blk,blk),1)
    allowed=rowi<=coli
    zero64=jnp.zeros((HD,blk),bf16)

    def block(i,_):
        qt=qT[i]; gt=gT[i]
        qh=[jnp.concatenate([qt[:HD],zero64],0),jnp.concatenate([zero64,qt[HD:]],0)]
        gh=[jnp.concatenate([gt[:HD],zero64],0),jnp.concatenate([zero64,gt[HD:]],0)]
        rows=pl.ds(pl.multiple_of(i*blk,blk),blk)
        q=qs[rows,:]; g=gs[rows,:]
        zq=jnp.zeros_like(q)
        qm=[jnp.where(first,q,zq),jnp.where(first,zq,q)]
        gm=[jnp.where(first,g,zq),jnp.where(first,zq,g)]
        def sA(j,m):
            kr=pl.ds(pl.multiple_of(j*blk,blk),blk)
            k=ks[kr,:]
            out=[]
            for h in range(2):
                s=dot(k,qh[h])
                es[h,kr,:]=s
                out.append(jnp.maximum(m[h],jnp.max(s.reshape(blk//8,8,blk),axis=0)))
            return tuple(out)
        m0=jnp.full((8,blk),-1e30,f32)
        k=ks[rows,:]
        m=[]
        for h in range(2):
            s=jnp.where(allowed,dot(k,qh[h]),-1e30)
            es[h,rows,:]=s
            m.append(jnp.max(s.reshape(blk//8,8,blk),axis=0))
        m=lax.fori_loop(0,i,sA,tuple(m))
        mk=[jnp.max(t,axis=0,keepdims=True)*kk for t in m]
        oT[...]=jnp.zeros_like(oT)
        def sB(j,l):
            kr=pl.ds(pl.multiple_of(j*blk,blk),blk)
            out=[]
            for h in range(2):
                e=jnp.exp2(es[h,kr,:]*kk-mk[h])
                es[h,kr,:]=e
                out.append(l[h]+jnp.sum(e.reshape(blk//8,8,blk),axis=0))
                oT[h*HD:(h+1)*HD,:]+=dot(vT[j,h*HD:(h+1)*HD,:],e.astype(bf16))
            return tuple(out)
        z=jnp.zeros((8,blk),f32)
        l=lax.fori_loop(0,i+1,sB,(z,z))
        r=[1.0/jnp.sum(t,axis=0,keepdims=True) for t in l]
        o=[oT[h*HD:(h+1)*HD,:]*r[h] for h in range(2)]
        D=[jnp.sum(o[h]*gt[h*HD:(h+1)*HD].astype(f32),axis=0,keepdims=True) for h in range(2)]
        oT[...]=jnp.concatenate(o,0)
        dqT[...]=jnp.zeros_like(dqT)
        def sC(j,_):
            kr=pl.ds(pl.multiple_of(j*blk,blk),blk)
            v=vs[kr,:]
            pb=[];db=[]
            for h in range(2):
                p=es[h,kr,:]*r[h]
                ds=(p*(dot(v,gh[h])-D[h])).astype(bf16)
                pb.append(p.astype(bf16)); db.append(ds)
                dqT[h*HD:(h+1)*HD,:]+=dot(kT[j,h*HD:(h+1)*HD,:],ds)
            dv[kr,:]+=dot(pb[0],gm[0])+dot(pb[1],gm[1])
            dk[kr,:]+=dot(db[0],qm[0])+dot(db[1],qm[1])
            return 0
        lax.fori_loop(0,i+1,sC,0)
        qs[rows,:]=(dqT[...].T*HD**-0.5).astype(bf16)
        gs[rows,:]=oT[...].T.astype(bf16)
        return 0
    lax.fori_loop(0,nb,block,0)
    for h in range(nb//2):
        for who,ref in ((c,keep),(1-c,send)):
            rows=pl.ds(pl.multiple_of((2*h+who)*blk,blk),blk)
            dst=slice(h*blk,(h+1)*blk)
            t=[tab[n,rows,:] for n in range(3)]
            ref[0,dst,:]=gs[rows,:]
            ref[1,dst,:]=turn(qs[rows,:].astype(f32),t,True).astype(bf16)
            ref[2,dst,:]=turn((dk[rows,:]*HD**-0.5).astype(bf16).astype(f32),t,True).astype(bf16)
            ref[3,dst,:]=dv[rows,:].astype(bf16)

def attention(c, own, par, gown, gpar, tab, pair, npair=1, blk=512):
    rows=own.shape[1]; length=2*rows
    nb=length//blk
    spec=pl.BlockSpec((3,rows,128),lambda p,c:(0,0,p+pair))
    gspec=pl.BlockSpec((rows,128),lambda p,c:(0,p+pair))
    ospec=pl.BlockSpec((4,rows,128),lambda p,c:(0,0,p))
    V=pltpu.VMEM
    return pl.pallas_call(
        functools.partial(attn_body,blk=blk,length=length),
        out_shape=(jax.ShapeDtypeStruct((4,rows,128*npair),bf16),)*2,
        grid_spec=pltpu.PrefetchScalarGridSpec(num_scalar_prefetch=1,grid=(npair,),
            in_specs=[spec,spec,gspec,gspec,pl.BlockSpec((3,length,128),lambda p,c:(0,0,0),pipeline_mode=pl.Buffered(1))],
            out_specs=[ospec,ospec],
            scratch_shapes=[V((length,128),bf16)]*4+[V((nb,128,blk),bf16)]*4+
              [V((2,length,blk),f32),V((128,blk),f32),V((128,blk),f32),V((length,128),f32),V((length,128),f32)]),
        compiler_params=pltpu.CompilerParams(vmem_limit_bytes=56<<20),
        name="attention",
        cost_estimate=pl.CostEstimate(flops=int(6*2*length*length//2*HD*2*npair*4),transcendentals=length*length*npair,bytes_accessed=16*rows*128*2*npair),
    )(c,own,par,gown,gpar,tab)
eps_norm = 1e-05
rope_base = 10000.0
EXTRA = 128

def dot_nt(a,b): return lax.dot_general(a,b,(((1,),(1,)),((),())),preferred_element_type=f32)
def dot_tn(a,b): return lax.dot_general(a,b,(((0,),(0,)),((),())),preferred_element_type=f32)

def norm_of(x):
    x=x.astype(f32)
    ce=x-jnp.mean(x,axis=-1,keepdims=True)
    inv=lax.rsqrt(jnp.mean(ce*ce,axis=-1,keepdims=True)+eps_norm)
    return ce*inv,inv

def norm_back(up,normed,inv,gain):
    s=up*gain
    return inv*(s-jnp.mean(s,axis=-1,keepdims=True)-normed*jnp.mean(s*normed,axis=-1,keepdims=True))

WHOLE=lambda shape: pl.BlockSpec(shape,lambda *a:(0,)*len(shape),pipeline_mode=pl.Buffered(1))

def pack_body(pk,ow,a,b,c,d,e,f,pb,eb,out,s):
    r=out.shape[0]
    s[...]=jnp.zeros_like(s)
    for k,v in enumerate((a,b,c,d,e,f)): s[k:k+1,0:r]=v[...].astype(f32)[None,:]
    s[6:9,0:r]=pb[...].astype(f32)
    ebv=eb[...].astype(f32)[None,:]
    for k in range(4): s[9+k:10+k,0:r]=ebv[:,k*r:(k+1)*r]
    out[:,:1536]=pk[:,:1536]
    out[:,1536:1536+EXTRA]=s[...].T[0:r,:].astype(bf16)
    out[:,1536+EXTRA:2304+EXTRA]=pk[:,1536:]
    out[:,2304+EXTRA:]=ow[...]
def pack(pk,ow,vecs,pb,eb):
    return pl.pallas_call(pack_body,out_shape=jax.ShapeDtypeStruct((pk.shape[0],3072+EXTRA),bf16),
        scratch_shapes=[pltpu.VMEM((EXTRA,128),f32)],name="pack")(pk,ow,*vecs,pb,eb)

def quarter(me_ref,n):
    return (me_ref[0]^(n//2))*2+(me_ref[1]^(n%2))

def rows_of(me_ref,n,q):
    return pl.ds(pl.multiple_of(quarter(me_ref,n)*q,q),q)

def split(c,value,keep,send,half):
    for k in range(2):
        @pl.when(c==k)
        def _():
            keep[...]=value[:,k*half:(k+1)*half]
            send[...]=value[:,(1-k)*half:(2-k)*half]

def proj_body(me, a, b, *refs):
    qa,qb=refs[:4],refs[4:8]
    tab,keep,send,t,vec,ws,ex=refs[8:]
    i=pl.program_id(0)
    @pl.when(i==0)
    def _():
        for n in range(4):
            rows=rows_of(me,n,qa[n].shape[0])
            ws[rows,:1536]=qa[n][:,:1536]
            ws[rows,1536:]=qb[n][...]
            ex[rows,:]=qa[n][:,1536:].astype(f32)
        vec[...]=ex[...].T[:16,:]
    x=jnp.where(i//2==me[0],a[0],b[...])
    t[...]=x
    normed,_=norm_of(x)
    b1=(normed*vec[0:1,:]+vec[1:2,:]).astype(bf16)
    tb=[tab[n] for n in range(3)]
    for j in range(3):
        v=dot(b1,ws[:,j*768:(j+1)*768])+vec[6+j:7+j,:]
        if j<2: v=jnp.concatenate([turn(v[:,g*128:(g+1)*128],tb,False) for g in range(6)],1)
        split(me[1],v.astype(bf16),keep.at[j],send.at[j],384)

def project(me,mine,other,qa,qb,tab,rb=256):
    n=2*other.shape[0]; per=n//2//rb
    S=jax.ShapeDtypeStruct
    out=pl.BlockSpec((3,rb,384),lambda i,me:(0,i,0))
    return pl.pallas_call(proj_body,
        out_shape=(S((3,n,384),bf16),S((3,n,384),bf16),S((n,768),bf16),S((16,768),f32)),
        grid_spec=pltpu.PrefetchScalarGridSpec(num_scalar_prefetch=1,grid=(n//rb,),
            in_specs=[pl.BlockSpec((1,rb,768),lambda i,me:(me[0],i%per,0)),pl.BlockSpec((rb,768),lambda i,me:(i%per,0))]+
              [WHOLE(w.shape) for w in qa]+[WHOLE((w.shape[0],768)) for w in qb]+
              [pl.BlockSpec((3,rb,128),lambda i,me:(0,(2*(i//per)+me[1])*per+i%per,0))],
            out_specs=(out,out,pl.BlockSpec((rb,768),lambda i,me:(i,0)),pl.BlockSpec((16,768),lambda i,me:(0,0))),
            scratch_shapes=[pltpu.VMEM((768,2304),bf16),pltpu.VMEM((768,EXTRA),f32)]),
        compiler_params=pltpu.CompilerParams(vmem_limit_bytes=56<<20),
        name="project",
        cost_estimate=pl.CostEstimate(flops=2*n*768*2304,transcendentals=n,bytes_accessed=n*768*10+768*3072*2),
    )(me,mine,other,*qa,*qb,tab)

def upst_body(me, a, b, *refs):
    qb,(keep,send,u,ws)=refs[:4],refs[4:]
    i=pl.program_id(0)
    @pl.when(i==0)
    def _():
        for n in range(4): ws[rows_of(me,n,qb[n].shape[0]),:]=qb[n][...]
    x=jnp.where(i//2==me[0],a[0],b[...])
    u[...]=x
    split(me[1],dot_nt(x,ws[...]).astype(bf16),keep,send,384)

def upstream_heads(me,mine,other,qb,rb=256):
    n=2*other.shape[0]; per=n//2//rb
    S=jax.ShapeDtypeStruct
    out=pl.BlockSpec((rb,384),lambda i,me:(i,0))
    return pl.pallas_call(upst_body,
        out_shape=(S((n,384),bf16),S((n,384),bf16),S((n,768),bf16)),
        grid_spec=pltpu.PrefetchScalarGridSpec(num_scalar_prefetch=1,grid=(n//rb,),
            in_specs=[pl.BlockSpec((1,rb,768),lambda i,me:(me[0],i%per,0)),pl.BlockSpec((rb,768),lambda i,me:(i%per,0))]+
              [pl.BlockSpec((w.shape[0],768),lambda i,me:(0,1),pipeline_mode=pl.Buffered(1)) for w in qb],
            out_specs=(out,out,pl.BlockSpec((rb,768),lambda i,me:(i,0))),
            scratch_shapes=[pltpu.VMEM((768,768),bf16)]),
        name="upstream",
        cost_estimate=pl.CostEstimate(flops=2*n*768*768,transcendentals=0,bytes_accessed=n*768*6+768*768*2),
    )(me,mine,other,*qb)

def outl_body(me, *refs):
    ka,ra,qb=refs[:3],refs[3:6],refs[6:10]
    mid,out,wos=refs[10:]
    @pl.when(pl.program_id(0)==0)
    def _():
        for n in range(4): wos[rows_of(me,n,qb[n].shape[0]),:]=qb[n][...]
    acc=mid[...]
    for g,a in ((0,ka),(1,ra)):
        rows=pl.ds(pl.multiple_of((me[1]^g)*384,384),384)
        acc=acc+dot(jnp.concatenate([r[0] for r in a],1),wos[rows,:])
    out[...]=acc.astype(bf16)

def layer_output(me,keep,recv,qb,mid,rb=256):
    n=mid.shape[0]
    a=pl.BlockSpec((1,rb,128),lambda i,me:(0,i,0))
    return pl.pallas_call(outl_body,
        out_shape=jax.ShapeDtypeStruct((n,768),bf16),
        grid_spec=pltpu.PrefetchScalarGridSpec(num_scalar_prefetch=1,grid=(n//rb,),
            in_specs=[a]*6+[pl.BlockSpec((w.shape[0],768),lambda i,me:(0,1),pipeline_mode=pl.Buffered(1)) for w in qb]+
              [pl.BlockSpec((rb,768),lambda i,me:(i,0))],
            out_specs=pl.BlockSpec((rb,768),lambda i,me:(i,0)),
            scratch_shapes=[pltpu.VMEM((768,768),bf16)]),
        name="layer_output",
        cost_estimate=pl.CostEstimate(flops=2*n*768*768,transcendentals=0,bytes_accessed=n*768*8+768*768*2),
    )(me,*keep,*recv,*qb,mid)

def back_body(me, *refs):
    ka,ra=refs[:3],refs[3:6]
    u,t,low=refs[6:9]
    qa,qb=refs[9:13],refs[13:17]
    vec,eb,sums_two,keepA,sendA,keepB,sendB,ig,ws,b1T,acc,gs,os,ex=refs[17:]
    g=pl.program_id(0)
    gc=me[1]^g
    @pl.when(g==0)
    def _():
        for i in range(4):
            rows=rows_of(me,i,qa[i].shape[0])
            for h in range(2):
                for j in range(2): ws[h,rows,j*384:(j+1)*384]=qa[i][:,(2*j+h)*384:(2*j+h+1)*384]
                ws[h,rows,768:1152]=qb[i][:,h*384:(h+1)*384]
        acc[...]=jnp.zeros_like(acc)
        ex[...]=jnp.zeros_like(ex)
        ex[4:5,:]=jnp.sum(u[...].astype(f32),axis=0,keepdims=True)
        ex[2:4,:]=sums_two[0:2,:]
        ex[8:12,:]=eb[...]
        normed,_=norm_of(t[...])
        b1T[...]=(normed*vec[0:1,:]+vec[1:2,:]).astype(bf16).T
    def one(a):
        p=jnp.concatenate([r[j] for j in (1,2,3) for r in a],1)
        acc[...]+=dot_nt(p,ws[gc])
        gs[...]=dot(b1T[...],p).astype(bf16)
        os[pl.ds(pl.multiple_of(gc*384,384),384),:]=dot_tn(jnp.concatenate([r[0] for r in a],1),u[...]).astype(bf16)
        s=jnp.sum(p.astype(f32),axis=0,keepdims=True)
        for h in range(2):
            @pl.when(gc==h)
            def _():
                for j in range(3): ex[5+j:6+j,h*384:(h+1)*384]=s[:,j*384:(j+1)*384]
    @pl.when(g==0)
    def _(): one(ka)
    @pl.when(g==1)
    def _(): one(ra)
    for h in range(2):
        @pl.when(gc==h)
        def _():
            for i in range(4):
                A,B=((keepA,keepB),(sendA,sendB))[i%2]
                r=gs[rows_of(me,i,192),:]
                for j in range(2): A[i//2,:,(2*j+h)*384:(2*j+h+1)*384]=r[:,j*384:(j+1)*384]
                B[i//2,:,h*384:(h+1)*384]=r[:,768:]
    @pl.when(g==1)
    def _():
        normed,inv=norm_of(t[...])
        b=acc[...]
        ex[0:1,:]=jnp.sum(b*normed,axis=0,keepdims=True)
        ex[1:2,:]=jnp.sum(b,axis=0,keepdims=True)
        ig[...]=(low[...]+norm_back(b,normed,inv,vec[0:1,:])).astype(bf16)
        acc[0:768,0:EXTRA]=ex[...].T
        for i in range(4):
            A,B=((keepA,keepB),(sendA,sendB))[i%2]
            rows=rows_of(me,i,192)
            B[i//2,:,768:]=os[rows,:]
            A[i//2,:,1536:]=acc[rows,0:EXTRA].astype(bf16)

def back(me,keep,recv,u,t,low,qa,qb,vec,eb,sums_two):
    n=t.shape[0]
    S=jax.ShapeDtypeStruct; V=pltpu.VMEM
    A,B=(2,192,1536+EXTRA),(2,192,1536)
    return pl.pallas_call(back_body,
        out_shape=(S(A,bf16),S(A,bf16),S(B,bf16),S(B,bf16),S((n,768),bf16)),
        grid_spec=pltpu.PrefetchScalarGridSpec(num_scalar_prefetch=1,grid=(2,),
            in_specs=[WHOLE((4,n,128))]*6+[WHOLE((n,768))]*3+
              [WHOLE(w.shape) for w in qa]+[WHOLE((w.shape[0],768)) for w in qb]+[WHOLE((16,768)),WHOLE((4,768)),WHOLE((8,768))],
            out_specs=[WHOLE(A),WHOLE(A),WHOLE(B),WHOLE(B),WHOLE((n,768))],
            scratch_shapes=[V((2,768,1152),bf16),V((768,n),bf16),V((n,768),f32),V((768,1152),bf16),V((768,768),bf16),V((EXTRA,768),f32)]),
        compiler_params=pltpu.CompilerParams(vmem_limit_bytes=58<<20),
        name="back",
        cost_estimate=pl.CostEstimate(flops=2*n*768*768*7,transcendentals=n,bytes_accessed=n*768*24+768*3072*6),
    )(me,*keep,*recv,u,t,low,*qa,*qb,vec,eb,sums_two)

def feed_body(me, t,u,e0,e1,e2,e3,r0,r1,r2,r3,be,vec, keepR,sendR,keepE,sendE,eb,mid,low,sums, b2,b2T,we,wr,act,hg,am,ab,egs, *, rb):
    s=pl.program_id(0)
    n=t.shape[0]; fb=we.shape[1]
    @pl.when(s==0)
    def _():
        def one(i,_):
            rows=pl.ds(pl.multiple_of(i*rb,rb),rb)
            normed,_=norm_of(t[rows,:])
            b=(normed*vec[2:3,:]+vec[3:4,:]).astype(bf16)
            b2[rows,:]=b
            b2T[i]=b.T
            am[rows,:]=t[rows,:].astype(f32)+(vec[4:5,:]+vec[5:6,:])
            ab[rows,:]=jnp.zeros((rb,768),f32)
            return 0
        lax.fori_loop(0,n//rb,one,0)
    for i,e in enumerate((e0,e1,e2,e3)): we[rows_of(me,i,192),:]=e[...]
    for i,r in enumerate((r0,r1,r2,r3)):
        @pl.when(s==i)
        def _(): wr[...]=r[...]
    w_e=we[...]; w_r=wr[...]
    def one(i,bs):
        rows=pl.ds(pl.multiple_of(i*rb,rb),rb)
        h=dot(b2[rows,:],w_e)+be[0]
        ag=dot_nt(u[rows,:],w_r)
        cdf=0.5+0.5*lax.erf(h*0.7071067811865476)
        a=(h*cdf).astype(bf16)
        d=(ag*(cdf+h*(0.3989422804014327*jnp.exp(h*h*-0.5)))).astype(bf16)
        act[rows,:]=a; hg[rows,:]=d
        am[rows,:]+=dot(a,w_r)
        ab[rows,:]+=dot_nt(d,w_e)
        return bs+jnp.sum(d.astype(f32).reshape(rb//8,8,fb),axis=0)
    bs=lax.fori_loop(0,n//rb,one,jnp.zeros((8,fb),f32))
    eb[0]=jnp.sum(bs,axis=0,keepdims=True)
    g=dot_tn(act[...],u[...]).astype(bf16)
    @pl.when(s%2==0)
    def _(): keepR[0]=g
    @pl.when(s%2==1)
    def _(): sendR[0]=g
    x=dot(b2T[0],hg[0:rb,:])
    for i in range(1,n//rb): x=x+dot(b2T[i],hg[i*rb:(i+1)*rb,:])
    egs[...]=x.astype(bf16)
    for i in range(4): (keepE,sendE)[i%2][i//2]=egs[rows_of(me,i,192),:]
    @pl.when(s==3)
    def _():
        def fin(i,c):
            rows=pl.ds(pl.multiple_of(i*rb,rb),rb)
            mid[rows,:]=am[rows,:]
            normed,inv=norm_of(t[rows,:])
            b=ab[rows,:]
            low[rows,:]=u[rows,:].astype(f32)+norm_back(b,normed,inv,vec[2:3,:])
            return c[0]+jnp.sum(b*normed,axis=0,keepdims=True),c[1]+jnp.sum(b,axis=0,keepdims=True)
        z=jnp.zeros((1,768),f32)
        p,q=lax.fori_loop(0,n//rb,fin,(z,z))
        sums[...]=jnp.zeros_like(sums)
        sums[0:1,:]=p; sums[1:2,:]=q

def feed(me,t,u,eq,rq,be,vec,rb=256):
    n=t.shape[0]; fb=768
    S=jax.ShapeDtypeStruct; V=pltpu.VMEM
    def qa(s,me): return (me[0]^(s//2))*2+(me[1]^(s%2))
    R=pl.BlockSpec((1,768,768),lambda s,me:(s//2,0,0))
    E=pl.BlockSpec((2,192,fb),lambda s,me:(0,0,qa(s,me)))
    return pl.pallas_call(functools.partial(feed_body,rb=rb),
        out_shape=[S((2,768,768),bf16)]*2+[S((2,192,4*fb),bf16)]*2+[S((4,1,fb),f32),S((n,768),f32),S((n,768),f32),S((8,768),f32)],
        grid_spec=pltpu.PrefetchScalarGridSpec(num_scalar_prefetch=1,grid=(4,),
            in_specs=[WHOLE((n,768))]*2+[pl.BlockSpec((192,fb),lambda s,me:(0,qa(s,me)))]*4+[WHOLE((768,768))]*4+
              [pl.BlockSpec((1,1,fb),lambda s,me:(qa(s,me),0,0)),WHOLE((16,768))],
            out_specs=[R,R,E,E,pl.BlockSpec((1,1,fb),lambda s,me:(qa(s,me),0,0))]+[WHOLE((n,768))]*2+[WHOLE((8,768))],
            scratch_shapes=[V((n,768),bf16),V((n//rb,768,rb),bf16),V((768,fb),bf16),V((fb,768),bf16),V((n,fb),bf16),V((n,fb),bf16),
                            V((n,768),f32),V((n,768),f32),V((768,fb),bf16)]),
        compiler_params=pltpu.CompilerParams(vmem_limit_bytes=60<<20),
        name="feed",
        cost_estimate=pl.CostEstimate(flops=6*2*n*768*4*fb,transcendentals=n*4*fb*2,bytes_accessed=n*768*20+768*fb*32),
    )(me,t,u,*eq,*rq,be,vec)

def finish_body(*refs):
    pieces,(packed,output,vecs)=refs[:-3],refs[-3:]
    total=pieces[0][...].astype(f32)
    for p in pieces[1:]: total=total+p[...].astype(f32)
    packed[:,:1536]=total[:,:1536]
    packed[:,1536:]=total[:,1536+EXTRA:2304+EXTRA]
    output[...]=total[:,2304+EXTRA:]
    vecs[...]=total[:,1536:1536+EXTRA].T

def finish(pieces):
    r=pieces[0].shape[0]
    S=jax.ShapeDtypeStruct
    return pl.pallas_call(finish_body,out_shape=(S((r,2304),f32),S((r,768),f32),S((EXTRA,r),f32)),name="finish")(*pieces)

def swap(a, axis):
    return lax.ppermute(a, axis, [(0, 1), (1, 0)])


def shift(a, axis, size, step):
    return lax.ppermute(a, axis, [(i, (i + step) % size) for i in range(size)])


def pick(index, here, there):
    place = lax.broadcasted_iota(jnp.int32, (2,) + (1,) * here.ndim, 0)
    return jnp.where(place == index, here[None], there[None])


def after(value, *others):
    return lax.optimization_barrier((value,) + others)[0]


def gather_line(shard, m):
    z = lax.axis_index("z")
    pieces = [shard] + [shift(shard, "z", m, step) for step in range(1, m)]
    back = (z - lax.broadcasted_iota(jnp.int32, (m,) + (1,) * shard.ndim, 0)) % m
    line = pieces[0][None]
    for step in range(1, m):
        line = jnp.where(back == step, pieces[step][None], line)
    return line


def join(y, near, far):
    return jnp.moveaxis(pick(y, near, far), 0, 1).reshape((-1,) + near.shape[2:])


def halve(a, y, m):
    a = a.reshape(a.shape[:-2] + (m, 2, -1) + a.shape[-1:])
    mine = lax.dynamic_index_in_dim(a, y, a.ndim - 3, keepdims=False)
    other = lax.dynamic_index_in_dim(a, 1 - y, a.ndim - 3, keepdims=False)
    return add(mine, swap(other, "y"), bf16)


def wide(a):
    a = a.reshape(a.shape[:-1] + (4, -1))
    return jnp.moveaxis(a, -2, -3).reshape(a.shape[:-3] + (-1, a.shape[-1]))


def narrow(a):
    a = a.reshape(a.shape[:-2] + (4, -1, a.shape[-1]))
    return jnp.moveaxis(a, -3, -2).reshape(a.shape[:-3] + (a.shape[-2], -1))


def add(a, b, dtype):
    return (a.astype(f32) + b.astype(f32)).astype(dtype)


def scatter_line(line, m):
    z = lax.axis_index("z")
    total = lax.dynamic_index_in_dim(line, z, 0, keepdims=False).astype(f32)
    for step in range(1, m):
        part = lax.dynamic_index_in_dim(line, (z + step) % m, 0, keepdims=False)
        total = total + shift(part, "z", m, step).astype(f32)
    return total


def rotary(length):
    half = ROT // 2
    frequency = rope_base ** (-(jnp.arange(half, dtype=f32) * 2.0 / ROT))
    lane = jnp.arange(128, dtype=jnp.int32) % HD
    angles = jnp.arange(length, dtype=jnp.int32).astype(f32)[:, None] * jnp.tile(frequency, 16)[None, :]
    co, si = jnp.cos(angles), jnp.sin(angles)
    return jnp.stack(
        [
            jnp.where(lane < ROT, co, 1.0),
            jnp.where(lane < half, -si, 0.0),
            jnp.where((lane >= half) & (lane < ROT), si, 0.0),
        ]
    )


def exchange(mine, x):
    other = swap(lax.dynamic_index_in_dim(mine, 1 - x, 0, keepdims=False), "x")
    place = lax.broadcasted_iota(jnp.int32, (2, 1, 1), 0)
    return jnp.where(place == x, mine, other[None])


def shards(
    inputs,
    first_gain,
    first_shift,
    second_gain,
    second_shift,
    packed_weight,
    packed_bias,
    output_weight,
    output_bias,
    expand_weight,
    expand_bias,
    reduce_weight,
    reduce_bias,
    cotangent,
    *,
    m,
):
    x, c, y = (lax.axis_index(a) for a in "xcy")
    me = jnp.stack([x, c]).astype(jnp.int32)
    block, width = inputs.shape[1:]
    r = first_gain.shape[0]
    first = 2 * width + EXTRA
    other_tokens = swap(lax.dynamic_index_in_dim(inputs, 1 - x, 0, keepdims=False), "x")
    vectors = [first_gain, first_shift, second_gain, second_shift, output_bias, reduce_bias]
    shard = pack(packed_weight, output_weight, vectors, packed_bias, expand_bias)
    table = rotary(4 * block)
    line = gather_line(shard, m)
    pair_r = jnp.stack([reduce_weight, swap(reduce_weight, "x")])
    line_a, line_b = line[:, :, :first], line[:, :, first:]
    far_b = swap(line_b, "x")
    near_a = join(y, line_a, swap(line_a, "y"))
    near_b = join(y, line_b, swap(line_b, "y"))
    far_a = swap(after(near_a, table), "x")
    far_b = join(y, far_b, swap(far_b, "y"))
    qa = [near_a, swap(near_a, "c"), far_a, swap(far_a, "c")]
    qb = [near_b, swap(near_b, "c"), far_b, swap(far_b, "c")]

    line_e = gather_line(expand_weight, m)
    line_r = gather_line(pair_r, m)
    other_grads = swap(lax.dynamic_index_in_dim(cotangent, 1 - x, 0, keepdims=False), "x")
    side_r = swap(line_r, "y")
    near_e = join(y, line_e, swap(line_e, "y"))

    own, send, t, vec = project(me, inputs, other_tokens, qa, qb, table)
    got = swap(send, "c")
    gown, gsend, u = upstream_heads(after(me, own), cotangent, other_grads, qb)
    ggot = swap(gsend, "c")
    core = me[1:]
    operands = (own, got, gown, ggot, table)
    keep0, give0 = attention(core, *operands, 0)

    near_r, far_r = (join(y, line_r[:, i], side_r[:, i]) for i in range(2))
    far_e = swap(near_e, "x")
    eq = [near_e, swap(near_e, "c"), far_e, swap(far_e, "c")]
    rq = [near_r, swap(near_r, "c"), far_r, swap(far_r, "c")]
    be = vec[9:13].reshape(4, -1, r).transpose(1, 0, 2).reshape(4, 1, -1)
    keep_r, send_r, keep_e, send_e, eb, mid, low, sums_two = feed(me, after(t, keep0), u, eq, rq, be, vec)
    eb = eb.reshape(-1, 4, r).transpose(1, 0, 2).reshape(4, width)
    keep1, give1 = attention(after(core, mid), *operands, 1)
    sum_r = add(keep_r, swap(send_r, "c"), bf16)
    sum_e = add(keep_e, swap(send_e, "c"), bf16)
    keep2, give2 = attention(after(core, keep1, sum_r, sum_e), *operands, 2)
    sum_r = add(sum_r[0], swap(sum_r[1], "x"), bf16)
    sum_e = halve(sum_e, y, m)
    keep = [keep0, keep1, keep2]
    recv = [swap(give0, "c"), swap(give1, "c"), swap(give2, "c")]
    layer_out = layer_output(after(me, sum_r, sum_e, keep2), keep, recv, qb, mid)
    sum_r = halve(sum_r, y, m)
    sum_e = add(sum_e[0], swap(sum_e[1], "x"), bf16)
    feed_line = jnp.stack([wide(sum_e), sum_r], 1)
    keep_a, send_a, keep_b, send_b, input_grad = back(
        after(me, layer_out, feed_line), keep, recv, u, t, low, qa, qb, vec, eb, sums_two
    )
    total = scatter_line(feed_line, m)
    expand_grad, reduce_grad = narrow(total[0]), total[1]
    layer_out = exchange(layer_out.reshape(inputs.shape), x)
    sum_a = add(keep_a, swap(send_a, "c"), bf16)
    sum_b = add(keep_b, swap(send_b, "c"), bf16)
    input_grad = exchange(input_grad.reshape(inputs.shape), x)
    line_a = halve(add(sum_a[0], swap(sum_a[1], "x"), bf16), y, m)
    sum_b = halve(sum_b, y, m)
    line_b = add(sum_b[0], swap(sum_b[1], "x"), bf16)
    line = jnp.concatenate([line_a, line_b], 2)
    z = lax.axis_index("z")
    pieces = [lax.dynamic_index_in_dim(line, (z + step) % m, 0, keepdims=False) for step in range(m)]
    pieces[1:] = [shift(p, "z", m, step + 1) for step, p in enumerate(pieces[1:])]
    packed_grad, output_grad, v = finish(pieces)
    return (
        layer_out,
        input_grad,
        v[0],
        v[1],
        v[2],
        v[3],
        packed_grad,
        v[5:8],
        output_grad,
        v[4],
        expand_grad,
        v[8:12].reshape(-1),
        reduce_grad,
        v[4],
    )


def solution(mesh):
    shard = mesh.shape["shard"]
    m = shard // 2
    fine = Mesh(mesh.devices.reshape(2, 2, m, 2), ("x", "c", "z", "y"))
    every = ("x", "c", "z", "y")
    tokens = P(("z", "y"), ("x", "c"), None)
    vec, mat = P(every), P(every, None)
    in_specs = (tokens, vec, vec, vec, vec, mat, P(None, every), mat, vec, mat, vec, mat, vec, tokens)
    out_specs = (tokens, tokens, vec, vec, vec, vec, mat, P(None, every), mat, vec, mat, vec, mat, vec)

    def body(*args):
        return shards(*args, m=m)

    return jax.shard_map(body, mesh=fine, in_specs=in_specs, out_specs=out_specs, check_vma=False)
```

```python
import functools
import jax, jax.numpy as jnp
from jax import lax
from jax.experimental import pallas as pl
from jax.experimental.pallas import tpu as pltpu
from jax.sharding import Mesh, PartitionSpec as P

HD=64
ROT=16
f32=jnp.float32; bf16=jnp.bfloat16

def dot(a,b): return jnp.dot(a,b,preferred_element_type=f32)

def turn(v,tab,back):
    sgn=-1.0 if back else 1.0
    return v*tab[0]+sgn*(pltpu.roll(v,120,1)*tab[1]+pltpu.roll(v,8,1)*tab[2])

def attn_body(c_ref, own, par, gown, gpar, tab, keep, send, qs, ks, gs, vs, qT, gT, kT, vT, es0, es1, eb, dss, mx0, mx1, oT, dqT, dk, dv, *, blk, length, ch):
    c=c_ref[0]
    nb=length//blk
    lane=lax.broadcasted_iota(jnp.int32,(1,128),1)
    first=lane<HD
    for j,(d,dT) in enumerate(((qs,qT),(ks,kT),(vs,vT),(gs,gT))):
        for h in range(nb//2):
            hr=slice(h*blk,(h+1)*blk)
            a,b=(own[j,hr,:],par[j,hr,:]) if j<3 else (gown[hr,:],gpar[hr,:])
            pa=pl.multiple_of((2*h+c)*blk,blk); pb=pl.multiple_of((2*h+1-c)*blk,blk)
            d[pl.ds(pa,blk),:]=a
            d[pl.ds(pb,blk),:]=b
            dT[2*h+c]=a.T
            dT[2*h+1-c]=b.T
    dk[...]=jnp.zeros_like(dk); dv[...]=jnp.zeros_like(dv)
    kk=HD**-0.5*1.4426950408889634
    zero64=jnp.zeros((HD,blk),bf16)
    nc=blk//ch

    def masked(x): return [jnp.concatenate([x[:HD],zero64],0),jnp.concatenate([zero64,x[HD:]],0)]
    def top(x): return jnp.max(x.reshape(x.shape[0]//8,8,blk),axis=0)

    def score_diag(i,qh,es,mx):
        coli=lax.broadcasted_iota(jnp.int32,(ch,blk),1)
        rowi=lax.broadcasted_iota(jnp.int32,(ch,blk),0)
        for a in range(nc):
            rows=pl.ds(pl.multiple_of(i*blk+a*ch,ch),ch)
            k=ks[rows,:]
            for h in range(2):
                s=jnp.where(rowi+a*ch<=coli,dot(k,qh[h]),-1e30)
                es[h,rows,:]=s
                mx[h]=jnp.maximum(mx[h],top(s))

    mx0[...]=jnp.full_like(mx0,-1e30)
    score_diag(0,masked(qT[0]),es0,mx0)

    def block(i,es,mx,es_next,mx_next):
        i1=jnp.minimum(i+1,nb-1)
        rows=pl.ds(pl.multiple_of(i*blk,blk),blk)
        q1=masked(qT[i1])
        mk=[jnp.max(mx[h],axis=0,keepdims=True)*kk for h in range(2)]
        mx_next[...]=jnp.full((2,8,blk),-1e30,f32)
        oT[...]=jnp.zeros_like(oT)
        def sB(j,l):
            out=list(l)
            for a in range(nc):
                kr=pl.ds(pl.multiple_of(j*blk+a*ch,ch),ch)
                k=ks[kr,:]
                for h in range(2):
                    s=dot(k,q1[h])
                    es_next[h,kr,:]=s
                    mx_next[h]=jnp.maximum(mx_next[h],top(s))
                    e=jnp.exp2(es[h,kr,:]*kk-mk[h])
                    es[h,kr,:]=e
                    eb[h,kr,:]=e.astype(bf16)
                    out[h]=out[h]+jnp.sum(e.reshape(ch//8,8,blk),axis=0)
            jr=pl.ds(pl.multiple_of(j*blk,blk),blk)
            for h in range(2):
                hs=slice(h*HD,(h+1)*HD)
                oT[hs,:]+=dot(vT[j,hs,:],eb[h,jr,:])
            return tuple(out)
        z=jnp.zeros((8,blk),f32)
        l=lax.fori_loop(0,i+1,sB,(z,z))
        @pl.when(i<nb-1)
        def _(): score_diag(i1,q1,es_next,mx_next)
        r=[1.0/jnp.sum(t,axis=0,keepdims=True) for t in l]
        gt=gT[i]
        sc=jnp.concatenate([(gt[h*HD:(h+1)*HD].astype(f32)*r[h]) for h in range(2)],0).astype(bf16)
        gh=masked(sc)
        o=[oT[h*HD:(h+1)*HD,:]*r[h] for h in range(2)]
        D=[jnp.sum(o[h]*sc[h*HD:(h+1)*HD].astype(f32),axis=0,keepdims=True) for h in range(2)]
        oT[...]=jnp.concatenate(o,0)
        g=sc.T
        q=qs[rows,:]
        zq=jnp.zeros_like(q)
        qm=[jnp.where(first,q,zq),jnp.where(first,zq,q)]
        gm=[jnp.where(first,g,zq),jnp.where(first,zq,g)]
        dqT[...]=jnp.zeros_like(dqT)
        def sC(j,_):
            for a in range(nc):
                kr=pl.ds(pl.multiple_of(j*blk+a*ch,ch),ch)
                v=vs[kr,:]
                ds=[(es[h,kr,:]*(dot(v,gh[h])-D[h])).astype(bf16) for h in range(2)]
                for h in range(2): dss[h,a*ch:(a+1)*ch,:]=ds[h]
                dv[kr,:]+=dot(eb[0,kr,:],gm[0])+dot(eb[1,kr,:],gm[1])
                dk[kr,:]+=dot(ds[0],qm[0])+dot(ds[1],qm[1])
            for h in range(2):
                hs=slice(h*HD,(h+1)*HD)
                dqT[hs,:]+=dot(kT[j,hs,:],dss[h])
            return 0
        lax.fori_loop(0,i+1,sC,0)
        qs[rows,:]=(dqT[...].T*HD**-0.5).astype(bf16)
        gs[rows,:]=oT[...].T.astype(bf16)

    def two(i,_):
        block(2*i,es0,mx0,es1,mx1)
        block(2*i+1,es1,mx1,es0,mx0)
        return 0
    lax.fori_loop(0,nb//2,two,0)
    for h in range(nb//2):
        for who,ref in ((c,keep),(1-c,send)):
            rows=pl.ds(pl.multiple_of((2*h+who)*blk,blk),blk)
            dst=slice(h*blk,(h+1)*blk)
            t=[tab[n,rows,:] for n in range(3)]
            ref[0,dst,:]=gs[rows,:]
            ref[1,dst,:]=turn(qs[rows,:].astype(f32),t,True).astype(bf16)
            ref[2,dst,:]=turn((dk[rows,:]*HD**-0.5).astype(bf16).astype(f32),t,True).astype(bf16)
            ref[3,dst,:]=dv[rows,:].astype(bf16)

def attention(c, own, par, gown, gpar, tab, pair, npair=1, blk=512, ch=512):
    rows=own.shape[1]; length=2*rows
    nb=length//blk
    spec=pl.BlockSpec((3,rows,128),lambda p,c:(0,0,p+pair))
    gspec=pl.BlockSpec((rows,128),lambda p,c:(0,p+pair))
    ospec=pl.BlockSpec((4,rows,128),lambda p,c:(0,0,p))
    V=pltpu.VMEM
    return pl.pallas_call(
        functools.partial(attn_body,blk=blk,length=length,ch=ch),
        out_shape=(jax.ShapeDtypeStruct((4,rows,128*npair),bf16),)*2,
        grid_spec=pltpu.PrefetchScalarGridSpec(num_scalar_prefetch=1,grid=(npair,),
            in_specs=[spec,spec,gspec,gspec,pl.BlockSpec((3,length,128),lambda p,c:(0,0,0),pipeline_mode=pl.Buffered(1))],
            out_specs=[ospec,ospec],
            scratch_shapes=[V((length,128),bf16)]*4+[V((nb,128,blk),bf16)]*4+
              [V((2,length,blk),f32),V((2,length,blk),f32),V((2,length,blk),bf16),V((2,blk,blk),bf16),V((2,8,blk),f32),V((2,8,blk),f32),
               V((128,blk),f32),V((128,blk),f32),V((length,128),f32),V((length,128),f32)]),
        compiler_params=pltpu.CompilerParams(vmem_limit_bytes=58<<20),
        name="attention",
        cost_estimate=pl.CostEstimate(flops=int(6*2*length*length//2*HD*2*npair*4),transcendentals=length*length*npair,bytes_accessed=16*rows*128*2*npair),
    )(c,own,par,gown,gpar,tab)
eps_norm = 1e-05
rope_base = 10000.0
EXTRA = 128

def dot_nt(a,b): return lax.dot_general(a,b,(((1,),(1,)),((),())),preferred_element_type=f32)
def dot_tn(a,b): return lax.dot_general(a,b,(((0,),(0,)),((),())),preferred_element_type=f32)

def norm_of(x):
    x=x.astype(f32)
    ce=x-jnp.mean(x,axis=-1,keepdims=True)
    inv=lax.rsqrt(jnp.mean(ce*ce,axis=-1,keepdims=True)+eps_norm)
    return ce*inv,inv

def norm_back(up,normed,inv,gain):
    s=up*gain
    return inv*(s-jnp.mean(s,axis=-1,keepdims=True)-normed*jnp.mean(s*normed,axis=-1,keepdims=True))

WHOLE=lambda shape: pl.BlockSpec(shape,lambda *a:(0,)*len(shape),pipeline_mode=pl.Buffered(1))

def pack_body(pk,ow,a,b,c,d,e,f,pb,eb,out,s):
    r=out.shape[0]
    s[...]=jnp.zeros_like(s)
    for k,v in enumerate((a,b,c,d,e,f)): s[k:k+1,0:r]=v[...].astype(f32)[None,:]
    s[6:9,0:r]=pb[...].astype(f32)
    ebv=eb[...].astype(f32)[None,:]
    for k in range(4): s[9+k:10+k,0:r]=ebv[:,k*r:(k+1)*r]
    out[:,:1536]=pk[:,:1536]
    out[:,1536:1536+EXTRA]=s[...].T[0:r,:].astype(bf16)
    out[:,1536+EXTRA:2304+EXTRA]=pk[:,1536:]
    out[:,2304+EXTRA:]=ow[...]
def pack(pk,ow,vecs,pb,eb):
    return pl.pallas_call(pack_body,out_shape=jax.ShapeDtypeStruct((pk.shape[0],3072+EXTRA),bf16),
        scratch_shapes=[pltpu.VMEM((EXTRA,128),f32)],name="pack")(pk,ow,*vecs,pb,eb)

def quarter(me_ref,n):
    return (me_ref[0]^(n//2))*2+(me_ref[1]^(n%2))

def rows_of(me_ref,n,q):
    return pl.ds(pl.multiple_of(quarter(me_ref,n)*q,q),q)

def split(c,value,keep,send,half):
    for k in range(2):
        @pl.when(c==k)
        def _():
            keep[...]=value[:,k*half:(k+1)*half]
            send[...]=value[:,(1-k)*half:(2-k)*half]

def proj_body(me, a, b, *refs):
    qa,qb=refs[:4],refs[4:8]
    tab,keep,send,t,vec,ws,ex,st=refs[8:]
    i=pl.program_id(0)
    @pl.when(i==0)
    def _():
        for n in range(4):
            rows=rows_of(me,n,qa[n].shape[0])
            ws[rows,:1536]=qa[n][:,:1536]
            ws[rows,1536:]=qb[n][...]
            ex[rows,:]=qa[n][:,1536:].astype(f32)
        vec[...]=ex[...].T[:16,:]
    x=jnp.where(i==me[0],a[0],b[...])
    t[...]=x
    normed,_=norm_of(x)
    b1=(normed*vec[0:1,:]+vec[1:2,:]).astype(bf16)
    half=x.shape[0]//2
    rows=[slice(r*half,(r+1)*half) for r in range(2)]
    vs=[[dot(b1[r,:],ws[:,j*768:(j+1)*768])+vec[6+j:7+j,:] for r in rows] for j in range(3)]
    for r in range(2):
        tb=[tab[n,rows[r],:] for n in range(3)]
        for j in range(2):
            for g in range(6): st[j,rows[r],g*128:(g+1)*128]=turn(vs[j][r][:,g*128:(g+1)*128],tb,False).astype(bf16)
        st[2,rows[r],:]=vs[2][r].astype(bf16)
    for k in range(2):
        @pl.when(me[1]==k)
        def _():
            keep[...]=st[:,:,k*384:(k+1)*384]
            send[...]=st[:,:,(1-k)*384:(2-k)*384]

def project(me,mine,other,qa,qb,tab):
    n=2*other.shape[0]; rb=n//2; per=1
    S=jax.ShapeDtypeStruct
    out=pl.BlockSpec((3,rb,384),lambda i,me:(0,i,0))
    return pl.pallas_call(proj_body,
        out_shape=(S((3,n,384),bf16),S((3,n,384),bf16),S((n,768),bf16),S((16,768),f32)),
        grid_spec=pltpu.PrefetchScalarGridSpec(num_scalar_prefetch=1,grid=(n//rb,),
            in_specs=[pl.BlockSpec((1,rb,768),lambda i,me:(me[0],i%per,0)),pl.BlockSpec((rb,768),lambda i,me:(i%per,0))]+
              [WHOLE(w.shape) for w in qa]+[WHOLE((w.shape[0],768)) for w in qb]+
              [pl.BlockSpec((3,rb,128),lambda i,me:(0,(2*(i//per)+me[1])*per+i%per,0))],
            out_specs=(out,out,pl.BlockSpec((rb,768),lambda i,me:(i,0)),pl.BlockSpec((16,768),lambda i,me:(0,0))),
            scratch_shapes=[pltpu.VMEM((768,2304),bf16),pltpu.VMEM((768,EXTRA),f32),pltpu.VMEM((3,rb,768),bf16)]),
        compiler_params=pltpu.CompilerParams(vmem_limit_bytes=56<<20),
        name="project",
        cost_estimate=pl.CostEstimate(flops=2*n*768*2304,transcendentals=n,bytes_accessed=n*768*10+768*3072*2),
    )(me,mine,other,*qa,*qb,tab)

def upst_body(me, a, b, *refs):
    qb,(keep,send,u,ws)=refs[:4],refs[4:]
    i=pl.program_id(0)
    @pl.when(i==0)
    def _():
        for n in range(4): ws[rows_of(me,n,qb[n].shape[0]),:]=qb[n][...]
    x=jnp.where(i==me[0],a[0],b[...])
    u[...]=x
    half=x.shape[0]//2
    split(me[1],jnp.concatenate([dot_nt(x[:half],ws[...]),dot_nt(x[half:],ws[...])],0).astype(bf16),keep,send,384)

def upstream_heads(me,mine,other,qb):
    n=2*other.shape[0]; rb=n//2; per=1
    S=jax.ShapeDtypeStruct
    out=pl.BlockSpec((rb,384),lambda i,me:(i,0))
    return pl.pallas_call(upst_body,
        out_shape=(S((n,384),bf16),S((n,384),bf16),S((n,768),bf16)),
        grid_spec=pltpu.PrefetchScalarGridSpec(num_scalar_prefetch=1,grid=(n//rb,),
            in_specs=[pl.BlockSpec((1,rb,768),lambda i,me:(me[0],i%per,0)),pl.BlockSpec((rb,768),lambda i,me:(i%per,0))]+
              [pl.BlockSpec((w.shape[0],768),lambda i,me:(0,1),pipeline_mode=pl.Buffered(1)) for w in qb],
            out_specs=(out,out,pl.BlockSpec((rb,768),lambda i,me:(i,0))),
            scratch_shapes=[pltpu.VMEM((768,768),bf16)]),
        name="upstream",
        cost_estimate=pl.CostEstimate(flops=2*n*768*768,transcendentals=0,bytes_accessed=n*768*6+768*768*2),
    )(me,mine,other,*qb)

def outl_body(me, *refs):
    ka,ra,qb=refs[:3],refs[3:6],refs[6:10]
    mid,out,wos=refs[10:]
    @pl.when(pl.program_id(0)==0)
    def _():
        for n in range(4): wos[rows_of(me,n,qb[n].shape[0]),:]=qb[n][...]
    half=mid.shape[0]//2
    for r in (slice(0,half),slice(half,2*half)):
        acc=mid[r,:]
        for g,a in ((0,ka),(1,ra)):
            rows=pl.ds(pl.multiple_of((me[1]^g)*384,384),384)
            acc=acc+dot(jnp.concatenate([p[0,r,:] for p in a],1),wos[rows,:])
        out[r,:]=acc.astype(bf16)

def layer_output(me,keep,recv,qb,mid,rb=512):
    n=mid.shape[0]
    a=pl.BlockSpec((1,rb,128),lambda i,me:(0,i,0))
    return pl.pallas_call(outl_body,
        out_shape=jax.ShapeDtypeStruct((n,768),bf16),
        grid_spec=pltpu.PrefetchScalarGridSpec(num_scalar_prefetch=1,grid=(n//rb,),
            in_specs=[a]*6+[pl.BlockSpec((w.shape[0],768),lambda i,me:(0,1),pipeline_mode=pl.Buffered(1)) for w in qb]+
              [pl.BlockSpec((rb,768),lambda i,me:(i,0))],
            out_specs=pl.BlockSpec((rb,768),lambda i,me:(i,0)),
            scratch_shapes=[pltpu.VMEM((768,768),bf16)]),
        name="layer_output",
        cost_estimate=pl.CostEstimate(flops=2*n*768*768,transcendentals=0,bytes_accessed=n*768*8+768*768*2),
    )(me,*keep,*recv,*qb,mid)

def back_body(me, *refs):
    ka,ra=refs[:3],refs[3:6]
    u,t,low=refs[6:9]
    qa,qb=refs[9:13],refs[13:17]
    vec,eb,sums_two,keepA,sendA,keepB,sendB,ig,ws,b1T,acc,gs,os,ex=refs[17:]
    g=pl.program_id(0)
    gc=me[1]^g
    @pl.when(g==0)
    def _():
        for i in range(4):
            rows=rows_of(me,i,qa[i].shape[0])
            for h in range(2):
                for j in range(2): ws[h,rows,j*384:(j+1)*384]=qa[i][:,(2*j+h)*384:(2*j+h+1)*384]
                ws[h,rows,768:1152]=qb[i][:,h*384:(h+1)*384]
        acc[...]=jnp.zeros_like(acc)
        ex[...]=jnp.zeros_like(ex)
        ex[4:5,:]=jnp.sum(u[...].astype(f32),axis=0,keepdims=True)
        ex[2:4,:]=sums_two[0:2,:]
        ex[8:12,:]=eb[...]
        normed,_=norm_of(t[...])
        b1T[...]=(normed*vec[0:1,:]+vec[1:2,:]).astype(bf16).T
    def one(a):
        p=jnp.concatenate([r[j] for j in (1,2,3) for r in a],1)
        acc[...]+=dot_nt(p,ws[gc])
        gs[...]=dot(b1T[...],p).astype(bf16)
        os[pl.ds(pl.multiple_of(gc*384,384),384),:]=dot_tn(jnp.concatenate([r[0] for r in a],1),u[...]).astype(bf16)
        s=jnp.sum(p.astype(f32),axis=0,keepdims=True)
        for h in range(2):
            @pl.when(gc==h)
            def _():
                for j in range(3): ex[5+j:6+j,h*384:(h+1)*384]=s[:,j*384:(j+1)*384]
    @pl.when(g==0)
    def _(): one(ka)
    @pl.when(g==1)
    def _(): one(ra)
    for h in range(2):
        @pl.when(gc==h)
        def _():
            for i in range(4):
                A,B=((keepA,keepB),(sendA,sendB))[i%2]
                r=gs[rows_of(me,i,192),:]
                for j in range(2): A[i//2,:,(2*j+h)*384:(2*j+h+1)*384]=r[:,j*384:(j+1)*384]
                B[i//2,:,h*384:(h+1)*384]=r[:,768:]
    @pl.when(g==1)
    def _():
        normed,inv=norm_of(t[...])
        b=acc[...]
        ex[0:1,:]=jnp.sum(b*normed,axis=0,keepdims=True)
        ex[1:2,:]=jnp.sum(b,axis=0,keepdims=True)
        ig[...]=(low[...]+norm_back(b,normed,inv,vec[0:1,:])).astype(bf16)
        acc[0:768,0:EXTRA]=ex[...].T
        for i in range(4):
            A,B=((keepA,keepB),(sendA,sendB))[i%2]
            rows=rows_of(me,i,192)
            B[i//2,:,768:]=os[rows,:]
            A[i//2,:,1536:]=acc[rows,0:EXTRA].astype(bf16)

def back(me,keep,recv,u,t,low,qa,qb,vec,eb,sums_two):
    n=t.shape[0]
    S=jax.ShapeDtypeStruct; V=pltpu.VMEM
    A,B=(2,192,1536+EXTRA),(2,192,1536)
    return pl.pallas_call(back_body,
        out_shape=(S(A,bf16),S(A,bf16),S(B,bf16),S(B,bf16),S((n,768),bf16)),
        grid_spec=pltpu.PrefetchScalarGridSpec(num_scalar_prefetch=1,grid=(2,),
            in_specs=[WHOLE((4,n,128))]*6+[WHOLE((n,768))]*3+
              [WHOLE(w.shape) for w in qa]+[WHOLE((w.shape[0],768)) for w in qb]+[WHOLE((16,768)),WHOLE((4,768)),WHOLE((8,768))],
            out_specs=[WHOLE(A),WHOLE(A),WHOLE(B),WHOLE(B),WHOLE((n,768))],
            scratch_shapes=[V((2,768,1152),bf16),V((768,n),bf16),V((n,768),f32),V((768,1152),bf16),V((768,768),bf16),V((EXTRA,768),f32)]),
        compiler_params=pltpu.CompilerParams(vmem_limit_bytes=58<<20),
        name="back",
        cost_estimate=pl.CostEstimate(flops=2*n*768*768*7,transcendentals=n,bytes_accessed=n*768*24+768*3072*6),
    )(me,*keep,*recv,u,t,low,*qa,*qb,vec,eb,sums_two)

def feed_body(me, t,u,e0,e1,e2,e3,r0,r1,r2,r3,be,vec, keepR,sendR,keepE,sendE,eb,mid,low,sums, b2,b2T,we,wr,act,hg,am,ab,egs,rgs, *, rb):
    s=pl.program_id(0)
    n=t.shape[0]; fb=we.shape[1]
    @pl.when(s==0)
    def _():
        def one(i,_):
            rows=pl.ds(pl.multiple_of(i*rb,rb),rb)
            normed,_=norm_of(t[rows,:])
            b=(normed*vec[2:3,:]+vec[3:4,:]).astype(bf16)
            b2[rows,:]=b
            b2T[i]=b.T
            am[rows,:]=t[rows,:].astype(f32)+(vec[4:5,:]+vec[5:6,:])
            ab[rows,:]=jnp.zeros((rb,768),f32)
            return 0
        lax.fori_loop(0,n//rb,one,0)
    for i,e in enumerate((e0,e1,e2,e3)): we[rows_of(me,i,192),:]=e[...]
    for i,r in enumerate((r0,r1,r2,r3)):
        @pl.when(s==i)
        def _(): wr[...]=r[...]
    def one(i,bs):
        rows=pl.ds(pl.multiple_of(i*rb,rb),rb)
        h=dot(b2[rows,:],we[...])+be[0]
        ag=dot_nt(u[rows,:],wr[...])
        cdf=0.5+0.5*lax.erf(h*0.7071067811865476)
        a=(h*cdf).astype(bf16)
        d=(ag*(cdf+h*(0.3989422804014327*jnp.exp(h*h*-0.5)))).astype(bf16)
        act[rows,:]=a; hg[rows,:]=d
        am[rows,:]+=dot(act[rows,:],wr[...])
        ab[rows,:]+=dot_nt(hg[rows,:],we[...])
        return bs+jnp.sum(d.astype(f32).reshape(rb//8,8,fb),axis=0)
    bs=lax.fori_loop(0,n//rb,one,jnp.zeros((8,fb),f32))
    eb[0]=jnp.sum(bs,axis=0,keepdims=True)
    rgs[...]=dot_tn(act[...],u[...]).astype(bf16)
    x=dot(b2T[0],hg[0:rb,:])
    for i in range(1,n//rb): x=x+dot(b2T[i],hg[i*rb:(i+1)*rb,:])
    egs[...]=x.astype(bf16)
    @pl.when(s%2==0)
    def _(): keepR[0]=rgs[...]
    @pl.when(s%2==1)
    def _(): sendR[0]=rgs[...]
    for i in range(4): (keepE,sendE)[i%2][i//2]=egs[rows_of(me,i,192),:]
    @pl.when(s==3)
    def _():
        def fin(i,c):
            rows=pl.ds(pl.multiple_of(i*rb,rb),rb)
            mid[rows,:]=am[rows,:]
            normed,inv=norm_of(t[rows,:])
            b=ab[rows,:]
            low[rows,:]=u[rows,:].astype(f32)+norm_back(b,normed,inv,vec[2:3,:])
            return c[0]+jnp.sum(b*normed,axis=0,keepdims=True),c[1]+jnp.sum(b,axis=0,keepdims=True)
        z=jnp.zeros((1,768),f32)
        p,q=lax.fori_loop(0,n//rb,fin,(z,z))
        sums[...]=jnp.zeros_like(sums)
        sums[0:1,:]=p; sums[1:2,:]=q

def feed(me,t,u,eq,rq,be,vec,rb=512):
    n=t.shape[0]; fb=768
    S=jax.ShapeDtypeStruct; V=pltpu.VMEM
    def qa(s,me): return (me[0]^(s//2))*2+(me[1]^(s%2))
    R=pl.BlockSpec((1,768,768),lambda s,me:(s//2,0,0))
    E=pl.BlockSpec((2,192,fb),lambda s,me:(0,0,qa(s,me)))
    return pl.pallas_call(functools.partial(feed_body,rb=rb),
        out_shape=[S((2,768,768),bf16)]*2+[S((2,192,4*fb),bf16)]*2+[S((4,1,fb),f32),S((n,768),f32),S((n,768),f32),S((8,768),f32)],
        grid_spec=pltpu.PrefetchScalarGridSpec(num_scalar_prefetch=1,grid=(4,),
            in_specs=[WHOLE((n,768))]*2+[pl.BlockSpec((192,fb),lambda s,me:(0,qa(s,me)))]*4+[WHOLE((768,768))]*4+
              [pl.BlockSpec((1,1,fb),lambda s,me:(qa(s,me),0,0)),WHOLE((16,768))],
            out_specs=[R,R,E,E,pl.BlockSpec((1,1,fb),lambda s,me:(qa(s,me),0,0))]+[WHOLE((n,768))]*2+[WHOLE((8,768))],
            scratch_shapes=[V((n,768),bf16),V((n//rb,768,rb),bf16),V((768,fb),bf16),V((fb,768),bf16),V((n,fb),bf16),V((n,fb),bf16),
                            V((n,768),f32),V((n,768),f32),V((768,fb),bf16),V((fb,768),bf16)]),
        compiler_params=pltpu.CompilerParams(vmem_limit_bytes=60<<20),
        name="feed",
        cost_estimate=pl.CostEstimate(flops=6*2*n*768*4*fb,transcendentals=n*4*fb*2,bytes_accessed=n*768*20+768*fb*32),
    )(me,t,u,*eq,*rq,be,vec)

def finish_body(*refs):
    pieces,(packed,output,expand,reduce_,*vecs)=refs[:-11],refs[-11:]
    count=len(pieces)//2
    r=packed.shape[0]
    def total(ps,*at):
        s=ps[0][at].astype(f32)
        for p in ps[1:]: s=s+p[at].astype(f32)
        return s
    s=total(pieces[:count],Ellipsis)
    packed[:,:1536]=s[:,:1536]
    packed[:,1536:]=s[:,1536+EXTRA:2304+EXTRA]
    output[...]=s[:,2304+EXTRA:]
    v=s[:,1536:1536+EXTRA].T
    for i in range(5): vecs[i][...]=v[i,:]
    vecs[5][...]=v[5:8,:]
    vecs[6][...]=jnp.concatenate([v[8+i:9+i,:] for i in range(4)],1)[0,:]
    e=total(pieces[count:],0)
    for i in range(4): expand[:,i*768:(i+1)*768]=e[i*r:(i+1)*r,:]
    reduce_[...]=total(pieces[count:],1)

def finish(pieces,feed_pieces):
    r=pieces[0].shape[0]
    S=jax.ShapeDtypeStruct
    o=pl.pallas_call(finish_body,out_shape=[S((r,2304),f32),S((r,768),f32),S((r,3072),f32),S((4*r,768),f32)]+[S((r,),f32)]*5+
        [S((3,r),f32),S((4*r,),f32)],name="finish")(*pieces,*feed_pieces)
    return o[:4],o[4:9],o[9],o[10]


def swap(a, axis):
    return lax.ppermute(a, axis, [(0, 1), (1, 0)])


def shift(a, axis, size, step):
    return lax.ppermute(a, axis, [(i, (i + step) % size) for i in range(size)])


def pick(index, here, there):
    place = lax.broadcasted_iota(jnp.int32, (2,) + (1,) * here.ndim, 0)
    return jnp.where(place == index, here[None], there[None])


def after(value, *others):
    return lax.optimization_barrier((value,) + others)[0]


def gather_line(shard, m):
    z = lax.axis_index("z")
    pieces = [shard] + [shift(shard, "z", m, step) for step in range(1, m)]
    back = (z - lax.broadcasted_iota(jnp.int32, (m,) + (1,) * shard.ndim, 0)) % m
    line = pieces[0][None]
    for step in range(1, m):
        line = jnp.where(back == step, pieces[step][None], line)
    return line


def join(y, near, far):
    return jnp.moveaxis(pick(y, near, far), 0, 1).reshape((-1,) + near.shape[2:])


def halve(a, y, m):
    a = a.reshape(a.shape[:-2] + (m, 2, -1) + a.shape[-1:])
    mine = lax.dynamic_index_in_dim(a, y, a.ndim - 3, keepdims=False)
    other = lax.dynamic_index_in_dim(a, 1 - y, a.ndim - 3, keepdims=False)
    return add(mine, swap(other, "y"), bf16)


def wide(a):
    a = a.reshape(a.shape[:-1] + (4, -1))
    return jnp.moveaxis(a, -2, -3).reshape(a.shape[:-3] + (-1, a.shape[-1]))


def add(a, b, dtype):
    return (a.astype(f32) + b.astype(f32)).astype(dtype)


def line_pieces(line, m):
    z = lax.axis_index("z")
    pieces = [lax.dynamic_index_in_dim(line, (z + step) % m, 0, keepdims=False) for step in range(m)]
    return pieces[:1] + [shift(p, "z", m, step + 1) for step, p in enumerate(pieces[1:])]


def rotary(length):
    half = ROT // 2
    frequency = rope_base ** (-(jnp.arange(half, dtype=f32) * 2.0 / ROT))
    lane = jnp.arange(128, dtype=jnp.int32) % HD
    angles = jnp.arange(length, dtype=jnp.int32).astype(f32)[:, None] * jnp.tile(frequency, 16)[None, :]
    co, si = jnp.cos(angles), jnp.sin(angles)
    return jnp.stack(
        [
            jnp.where(lane < ROT, co, 1.0),
            jnp.where(lane < half, -si, 0.0),
            jnp.where((lane >= half) & (lane < ROT), si, 0.0),
        ]
    )


def exchange(mine, x):
    other = swap(lax.dynamic_index_in_dim(mine, 1 - x, 0, keepdims=False), "x")
    place = lax.broadcasted_iota(jnp.int32, (2, 1, 1), 0)
    return jnp.where(place == x, mine, other[None])


def shards(
    inputs,
    first_gain,
    first_shift,
    second_gain,
    second_shift,
    packed_weight,
    packed_bias,
    output_weight,
    output_bias,
    expand_weight,
    expand_bias,
    reduce_weight,
    reduce_bias,
    cotangent,
    *,
    m,
):
    x, c, y = (lax.axis_index(a) for a in "xcy")
    me = jnp.stack([x, c]).astype(jnp.int32)
    block, width = inputs.shape[1:]
    r = first_gain.shape[0]
    first = 2 * width + EXTRA
    other_tokens = swap(lax.dynamic_index_in_dim(inputs, 1 - x, 0, keepdims=False), "x")
    vectors = [first_gain, first_shift, second_gain, second_shift, output_bias, reduce_bias]
    shard = pack(packed_weight, output_weight, vectors, packed_bias, expand_bias)
    table = rotary(4 * block)
    line = gather_line(shard, m)
    pair_r = jnp.stack([reduce_weight, swap(reduce_weight, "x")])
    line_a, line_b = line[:, :, :first], line[:, :, first:]
    far_b = swap(line_b, "x")
    near_a = join(y, line_a, swap(line_a, "y"))
    near_b = join(y, line_b, swap(line_b, "y"))
    far_a = swap(after(near_a, table), "x")
    far_b = join(y, far_b, swap(far_b, "y"))
    qa = [near_a, swap(near_a, "c"), far_a, swap(far_a, "c")]
    qb = [near_b, swap(near_b, "c"), far_b, swap(far_b, "c")]

    line_e = gather_line(expand_weight, m)
    line_r = gather_line(pair_r, m)
    other_grads = swap(lax.dynamic_index_in_dim(cotangent, 1 - x, 0, keepdims=False), "x")
    side_r = swap(line_r, "y")
    near_e = join(y, line_e, swap(line_e, "y"))

    own, send, t, vec = project(me, inputs, other_tokens, qa, qb, table)
    got = swap(send, "c")
    gown, gsend, u = upstream_heads(after(me, own), cotangent, other_grads, qb)
    ggot = swap(gsend, "c")
    core = me[1:]
    operands = (own, got, gown, ggot, table)
    keep0, give0 = attention(core, *operands, 0)

    near_r, far_r = (join(y, line_r[:, i], side_r[:, i]) for i in range(2))
    far_e = swap(near_e, "x")
    eq = [near_e, swap(near_e, "c"), far_e, swap(far_e, "c")]
    rq = [near_r, swap(near_r, "c"), far_r, swap(far_r, "c")]
    be = vec[9:13].reshape(4, -1, r).transpose(1, 0, 2).reshape(4, 1, -1)
    keep_r, send_r, keep_e, send_e, eb, mid, low, sums_two = feed(me, after(t, keep0), u, eq, rq, be, vec)
    eb = eb.reshape(-1, 4, r).transpose(1, 0, 2).reshape(4, width)
    keep1, give1 = attention(after(core, mid), *operands, 1)
    sum_r = add(keep_r, swap(send_r, "c"), bf16)
    sum_e = add(keep_e, swap(send_e, "c"), bf16)
    keep2, give2 = attention(after(core, keep1, sum_r, sum_e), *operands, 2)
    sum_r = add(sum_r[0], swap(sum_r[1], "x"), bf16)
    sum_e = halve(sum_e, y, m)
    keep = [keep0, keep1, keep2]
    recv = [swap(give0, "c"), swap(give1, "c"), swap(give2, "c")]
    layer_out = layer_output(after(me, sum_r, sum_e, keep2), keep, recv, qb, mid)
    sum_r = halve(sum_r, y, m)
    sum_e = add(sum_e[0], swap(sum_e[1], "x"), bf16)
    feed_line = jnp.stack([wide(sum_e), sum_r], 1)
    keep_a, send_a, keep_b, send_b, input_grad = back(
        after(me, layer_out), keep, recv, u, t, low, qa, qb, vec, eb, sums_two
    )
    feed_pieces = line_pieces(feed_line, m)
    layer_out = exchange(layer_out.reshape(inputs.shape), x)
    sum_a = add(keep_a, swap(send_a, "c"), bf16)
    sum_b = add(keep_b, swap(send_b, "c"), bf16)
    line_a = halve(add(sum_a[0], swap(sum_a[1], "x"), bf16), y, m)
    sum_b = halve(sum_b, y, m)
    line_b = add(sum_b[0], swap(sum_b[1], "x"), bf16)
    input_grad = exchange(after(input_grad, layer_out).reshape(inputs.shape), x)
    line = jnp.concatenate([line_a, line_b], 2)
    mats, v, packed_vec, expand_vec = finish(line_pieces(line, m), feed_pieces)
    packed_grad, output_grad, expand_grad, reduce_grad = mats
    return (
        layer_out,
        input_grad,
        v[0],
        v[1],
        v[2],
        v[3],
        packed_grad,
        packed_vec,
        output_grad,
        v[4],
        expand_grad,
        expand_vec,
        reduce_grad,
        v[4],
    )


def solution(mesh):
    shard = mesh.shape["shard"]
    m = shard // 2
    fine = Mesh(mesh.devices.reshape(2, 2, m, 2), ("x", "c", "z", "y"))
    every = ("x", "c", "z", "y")
    tokens = P(("z", "y"), ("x", "c"), None)
    vec, mat = P(every), P(every, None)
    in_specs = (tokens, vec, vec, vec, vec, mat, P(None, every), mat, vec, mat, vec, mat, vec, tokens)
    out_specs = (tokens, tokens, vec, vec, vec, vec, mat, P(None, every), mat, vec, mat, vec, mat, vec)

    def body(*args):
        return shards(*args, m=m)

    return jax.shard_map(body, mesh=fine, in_specs=in_specs, out_specs=out_specs, check_vma=False)
```

```python
import functools
import jax, jax.numpy as jnp
from jax import lax
from jax.experimental import pallas as pl
from jax.experimental.pallas import tpu as pltpu
from jax.sharding import Mesh, PartitionSpec as P

HD=64
ROT=16
f32=jnp.float32; bf16=jnp.bfloat16

def dot(a,b): return jnp.dot(a,b,preferred_element_type=f32)

def turn(v,tab,back):
    sgn=-1.0 if back else 1.0
    return v*tab[0]+sgn*(pltpu.roll(v,120,1)*tab[1]+pltpu.roll(v,8,1)*tab[2])

def attn_body(c_ref, own, par, gown, gpar, tab, keep, send, qs, ks, gs, vs, qT, gT, kT, vT, es0, es1, eb, dss, mx0, mx1, oT, dqT, dk, dv, *, blk, length, ch):
    c=c_ref[0]
    nb=length//blk
    lane=lax.broadcasted_iota(jnp.int32,(1,128),1)
    first=lane<HD
    for j,(d,dT) in enumerate(((qs,qT),(ks,kT),(vs,vT),(gs,gT))):
        for h in range(nb//2):
            hr=slice(h*blk,(h+1)*blk)
            a,b=(own[j,hr,:],par[j,hr,:]) if j<3 else (gown[hr,:],gpar[hr,:])
            pa=pl.multiple_of((2*h+c)*blk,blk); pb=pl.multiple_of((2*h+1-c)*blk,blk)
            d[pl.ds(pa,blk),:]=a
            d[pl.ds(pb,blk),:]=b
            dT[2*h+c]=a.T
            dT[2*h+1-c]=b.T
    dk[...]=jnp.zeros_like(dk); dv[...]=jnp.zeros_like(dv)
    kk=HD**-0.5*1.4426950408889634
    zero64=jnp.zeros((HD,blk),bf16)
    nc=blk//ch

    def masked(x): return [jnp.concatenate([x[:HD],zero64],0),jnp.concatenate([zero64,x[HD:]],0)]
    def top(x): return jnp.max(x.reshape(x.shape[0]//8,8,blk),axis=0)

    def score_diag(i,qh,es,mx):
        coli=lax.broadcasted_iota(jnp.int32,(ch,blk),1)
        rowi=lax.broadcasted_iota(jnp.int32,(ch,blk),0)
        for a in range(nc):
            rows=pl.ds(pl.multiple_of(i*blk+a*ch,ch),ch)
            k=ks[rows,:]
            for h in range(2):
                s=jnp.where(rowi+a*ch<=coli,dot(k,qh[h]),-1e30)
                es[h,rows,:]=s
                mx[h]=jnp.maximum(mx[h],top(s))

    mx0[...]=jnp.full_like(mx0,-1e30)
    score_diag(0,masked(qT[0]),es0,mx0)

    def block(i,es,mx,es_next,mx_next):
        i1=jnp.minimum(i+1,nb-1)
        rows=pl.ds(pl.multiple_of(i*blk,blk),blk)
        q1=masked(qT[i1])
        mk=[jnp.max(mx[h],axis=0,keepdims=True)*kk for h in range(2)]
        mx_next[...]=jnp.full((2,8,blk),-1e30,f32)
        oT[...]=jnp.zeros_like(oT)
        def sB(j,l):
            out=list(l)
            for a in range(nc):
                kr=pl.ds(pl.multiple_of(j*blk+a*ch,ch),ch)
                k=ks[kr,:]
                for h in range(2):
                    s=dot(k,q1[h])
                    es_next[h,kr,:]=s
                    mx_next[h]=jnp.maximum(mx_next[h],top(s))
                    e=jnp.exp2(es[h,kr,:]*kk-mk[h])
                    es[h,kr,:]=e
                    eb[h,kr,:]=e.astype(bf16)
                    out[h]=out[h]+jnp.sum(e.reshape(ch//8,8,blk),axis=0)
            jr=pl.ds(pl.multiple_of(j*blk,blk),blk)
            for h in range(2):
                hs=slice(h*HD,(h+1)*HD)
                oT[hs,:]+=dot(vT[j,hs,:],eb[h,jr,:])
            return tuple(out)
        z=jnp.zeros((8,blk),f32)
        l=lax.fori_loop(0,i+1,sB,(z,z))
        @pl.when(i<nb-1)
        def _(): score_diag(i1,q1,es_next,mx_next)
        r=[1.0/jnp.sum(t,axis=0,keepdims=True) for t in l]
        gt=gT[i]
        sc=jnp.concatenate([(gt[h*HD:(h+1)*HD].astype(f32)*r[h]) for h in range(2)],0).astype(bf16)
        gh=masked(sc)
        o=[oT[h*HD:(h+1)*HD,:]*r[h] for h in range(2)]
        D=[jnp.sum(o[h]*sc[h*HD:(h+1)*HD].astype(f32),axis=0,keepdims=True) for h in range(2)]
        oT[...]=jnp.concatenate(o,0)
        g=sc.T
        q=qs[rows,:]
        zq=jnp.zeros_like(q)
        qm=[jnp.where(first,q,zq),jnp.where(first,zq,q)]
        gm=[jnp.where(first,g,zq),jnp.where(first,zq,g)]
        dqT[...]=jnp.zeros_like(dqT)
        def sC(j,_):
            for a in range(nc):
                kr=pl.ds(pl.multiple_of(j*blk+a*ch,ch),ch)
                v=vs[kr,:]
                ds=[(es[h,kr,:]*(dot(v,gh[h])-D[h])).astype(bf16) for h in range(2)]
                for h in range(2): dss[h,a*ch:(a+1)*ch,:]=ds[h]
                dv[kr,:]+=dot(eb[0,kr,:],gm[0])+dot(eb[1,kr,:],gm[1])
                dk[kr,:]+=dot(ds[0],qm[0])+dot(ds[1],qm[1])
            for h in range(2):
                hs=slice(h*HD,(h+1)*HD)
                dqT[hs,:]+=dot(kT[j,hs,:],dss[h])
            return 0
        lax.fori_loop(0,i+1,sC,0)
        qs[rows,:]=(dqT[...].T*HD**-0.5).astype(bf16)
        gs[rows,:]=oT[...].T.astype(bf16)

    def two(i,_):
        block(2*i,es0,mx0,es1,mx1)
        block(2*i+1,es1,mx1,es0,mx0)
        return 0
    lax.fori_loop(0,nb//2,two,0)
    for h in range(nb//2):
        for who,ref in ((c,keep),(1-c,send)):
            rows=pl.ds(pl.multiple_of((2*h+who)*blk,blk),blk)
            dst=slice(h*blk,(h+1)*blk)
            t=[tab[n,rows,:] for n in range(3)]
            ref[0,dst,:]=gs[rows,:]
            ref[1,dst,:]=turn(qs[rows,:].astype(f32),t,True).astype(bf16)
            ref[2,dst,:]=turn((dk[rows,:]*HD**-0.5).astype(bf16).astype(f32),t,True).astype(bf16)
            ref[3,dst,:]=dv[rows,:].astype(bf16)

def attention(c, own, par, gown, gpar, tab, pair, npair=1, blk=512, ch=512):
    rows=own.shape[1]; length=2*rows
    nb=length//blk
    spec=pl.BlockSpec((3,rows,128),lambda p,c:(0,0,p+pair))
    gspec=pl.BlockSpec((rows,128),lambda p,c:(0,p+pair))
    ospec=pl.BlockSpec((4,rows,128),lambda p,c:(0,0,p))
    V=pltpu.VMEM
    return pl.pallas_call(
        functools.partial(attn_body,blk=blk,length=length,ch=ch),
        out_shape=(jax.ShapeDtypeStruct((4,rows,128*npair),bf16),)*2,
        grid_spec=pltpu.PrefetchScalarGridSpec(num_scalar_prefetch=1,grid=(npair,),
            in_specs=[spec,spec,gspec,gspec,pl.BlockSpec((3,length,128),lambda p,c:(0,0,0),pipeline_mode=pl.Buffered(1))],
            out_specs=[ospec,ospec],
            scratch_shapes=[V((length,128),bf16)]*4+[V((nb,128,blk),bf16)]*4+
              [V((2,length,blk),f32),V((2,length,blk),f32),V((2,length,blk),bf16),V((2,blk,blk),bf16),V((2,8,blk),f32),V((2,8,blk),f32),
               V((128,blk),f32),V((128,blk),f32),V((length,128),f32),V((length,128),f32)]),
        compiler_params=pltpu.CompilerParams(vmem_limit_bytes=58<<20),
        name="attention",
        cost_estimate=pl.CostEstimate(flops=int(6*2*length*length//2*HD*2*npair*4),transcendentals=length*length*npair,bytes_accessed=16*rows*128*2*npair),
    )(c,own,par,gown,gpar,tab)
eps_norm = 1e-05
rope_base = 10000.0
EXTRA = 128
BIAS = 32

def dot_nt(a,b): return lax.dot_general(a,b,(((1,),(1,)),((),())),preferred_element_type=f32)
def dot_tn(a,b): return lax.dot_general(a,b,(((0,),(0,)),((),())),preferred_element_type=f32)

def norm_of(x):
    x=x.astype(f32)
    ce=x-jnp.mean(x,axis=-1,keepdims=True)
    inv=lax.rsqrt(jnp.mean(ce*ce,axis=-1,keepdims=True)+eps_norm)
    return ce*inv,inv

def norm_back(up,normed,inv,gain):
    s=up*gain
    return inv*(s-jnp.mean(s,axis=-1,keepdims=True)-normed*jnp.mean(s*normed,axis=-1,keepdims=True))

WHOLE=lambda shape: pl.BlockSpec(shape,lambda *a:(0,)*len(shape),pipeline_mode=pl.Buffered(1))

def pack_body(pk,ow,a,b,c,d,e,f,pb,eb,out,s):
    r=out.shape[0]
    s[...]=jnp.zeros_like(s)
    for k,v in enumerate((a,b,c,d,e,f)): s[k:k+1,0:r]=v[...].astype(f32)[None,:]
    s[6:9,0:r]=pb[...].astype(f32)
    out[:,:1536]=pk[:,:1536]
    s[...]=s[...].T
    s[0:1,BIAS:BIAS+4*r]=eb[...].astype(f32)[None,:]
    out[:,1536:1536+EXTRA]=s[0:r,:].astype(bf16)
    out[:,1536+EXTRA:2304+EXTRA]=pk[:,1536:]
    out[:,2304+EXTRA:]=ow[...]
def pack(pk,ow,vecs,pb,eb):
    return pl.pallas_call(pack_body,out_shape=jax.ShapeDtypeStruct((pk.shape[0],3072+EXTRA),bf16),
        scratch_shapes=[pltpu.VMEM((EXTRA,128),f32)],name="pack")(pk,ow,*vecs,pb,eb)

def quarter(me_ref,n):
    return (me_ref[0]^(n//2))*2+(me_ref[1]^(n%2))

def rows_of(me_ref,n,q):
    return pl.ds(pl.multiple_of(quarter(me_ref,n)*q,q),q)

def split(c,value,keep,send,half):
    for k in range(2):
        @pl.when(c==k)
        def _():
            keep[...]=value[:,k*half:(k+1)*half]
            send[...]=value[:,(1-k)*half:(2-k)*half]

def proj_body(me, a, b, *refs, r_of):
    qa,qb=refs[:4],refs[4:8]
    tab,keep,send,t,vec,be,ws,ex,st=refs[8:]
    i=pl.program_id(0)
    @pl.when(i==0)
    def _():
        for n in range(4):
            rows=rows_of(me,n,qa[n].shape[0])
            ws[rows,:1536]=qa[n][:,:1536]
            ws[rows,1536:]=qb[n][...]
            ex[rows,:]=qa[n][:,1536:].astype(f32)
        vec[...]=ex[...].T[:16,:]
        per=4*r_of
        for d in range(3072//per):
            q,o=divmod(d*per,768)
            be[q,:,o:o+per]=ex[d*r_of:d*r_of+1,BIAS:BIAS+per]
    x=jnp.where(i==me[0],a[0],b[...])
    t[...]=x
    normed,_=norm_of(x)
    b1=(normed*vec[0:1,:]+vec[1:2,:]).astype(bf16)
    half=x.shape[0]//2
    rows=[slice(r*half,(r+1)*half) for r in range(2)]
    vs=[[dot(b1[r,:],ws[:,j*768:(j+1)*768])+vec[6+j:7+j,:] for r in rows] for j in range(3)]
    for r in range(2):
        tb=[tab[n,rows[r],:] for n in range(3)]
        for j in range(2):
            for g in range(6): st[j,rows[r],g*128:(g+1)*128]=turn(vs[j][r][:,g*128:(g+1)*128],tb,False).astype(bf16)
        st[2,rows[r],:]=vs[2][r].astype(bf16)
    for k in range(2):
        @pl.when(me[1]==k)
        def _():
            keep[...]=st[:,:,k*384:(k+1)*384]
            send[...]=st[:,:,(1-k)*384:(2-k)*384]

def project(me,mine,other,qa,qb,tab,r):
    n=2*other.shape[0]; rb=n//2; per=1
    S=jax.ShapeDtypeStruct
    out=pl.BlockSpec((3,rb,384),lambda i,me:(0,i,0))
    return pl.pallas_call(functools.partial(proj_body,r_of=r),
        out_shape=(S((3,n,384),bf16),S((3,n,384),bf16),S((n,768),bf16),S((16,768),f32),S((4,1,768),f32)),
        grid_spec=pltpu.PrefetchScalarGridSpec(num_scalar_prefetch=1,grid=(n//rb,),
            in_specs=[pl.BlockSpec((1,rb,768),lambda i,me:(me[0],i%per,0)),pl.BlockSpec((rb,768),lambda i,me:(i%per,0))]+
              [WHOLE(w.shape) for w in qa]+[WHOLE((w.shape[0],768)) for w in qb]+
              [pl.BlockSpec((3,rb,128),lambda i,me:(0,(2*(i//per)+me[1])*per+i%per,0))],
            out_specs=(out,out,pl.BlockSpec((rb,768),lambda i,me:(i,0)),pl.BlockSpec((16,768),lambda i,me:(0,0)),pl.BlockSpec((4,1,768),lambda i,me:(0,0,0))),
            scratch_shapes=[pltpu.VMEM((768,2304),bf16),pltpu.VMEM((768,EXTRA),f32),pltpu.VMEM((3,rb,768),bf16)]),
        compiler_params=pltpu.CompilerParams(vmem_limit_bytes=56<<20),
        name="project",
        cost_estimate=pl.CostEstimate(flops=2*n*768*2304,transcendentals=n,bytes_accessed=n*768*10+768*3072*2),
    )(me,mine,other,*qa,*qb,tab)

def upst_body(me, a, b, *refs):
    qb,(keep,send,u,ws)=refs[:4],refs[4:]
    i=pl.program_id(0)
    @pl.when(i==0)
    def _():
        for n in range(4): ws[rows_of(me,n,qb[n].shape[0]),:]=qb[n][...]
    x=jnp.where(i==me[0],a[0],b[...])
    u[...]=x
    half=x.shape[0]//2
    split(me[1],jnp.concatenate([dot_nt(x[:half],ws[...]),dot_nt(x[half:],ws[...])],0).astype(bf16),keep,send,384)

def upstream_heads(me,mine,other,qb):
    n=2*other.shape[0]; rb=n//2; per=1
    S=jax.ShapeDtypeStruct
    out=pl.BlockSpec((rb,384),lambda i,me:(i,0))
    return pl.pallas_call(upst_body,
        out_shape=(S((n,384),bf16),S((n,384),bf16),S((n,768),bf16)),
        grid_spec=pltpu.PrefetchScalarGridSpec(num_scalar_prefetch=1,grid=(n//rb,),
            in_specs=[pl.BlockSpec((1,rb,768),lambda i,me:(me[0],i%per,0)),pl.BlockSpec((rb,768),lambda i,me:(i%per,0))]+
              [pl.BlockSpec((w.shape[0],768),lambda i,me:(0,1),pipeline_mode=pl.Buffered(1)) for w in qb],
            out_specs=(out,out,pl.BlockSpec((rb,768),lambda i,me:(i,0))),
            scratch_shapes=[pltpu.VMEM((768,768),bf16)]),
        name="upstream",
        cost_estimate=pl.CostEstimate(flops=2*n*768*768,transcendentals=0,bytes_accessed=n*768*6+768*768*2),
    )(me,mine,other,*qb)

def outl_body(me, *refs):
    ka,ra,qb=refs[:3],refs[3:6],refs[6:10]
    mid,mine,other,wos=refs[10:]
    i=pl.program_id(0)
    @pl.when(i==0)
    def _():
        for n in range(4): wos[rows_of(me,n,qb[n].shape[0]),:]=qb[n][...]
    half=mid.shape[0]//2
    outs=[]
    for r in (slice(0,half),slice(half,2*half)):
        acc=mid[r,:]
        for g,a in ((0,ka),(1,ra)):
            rows=pl.ds(pl.multiple_of((me[1]^g)*384,384),384)
            acc=acc+dot(jnp.concatenate([p[0,r,:] for p in a],1),wos[rows,:])
        outs.append(acc.astype(bf16))
    out=jnp.concatenate(outs,0)
    @pl.when(i==me[0])
    def _(): mine[...]=out
    @pl.when(i!=me[0])
    def _(): other[...]=out

def layer_output(me,keep,recv,qb,mid):
    n=mid.shape[0]; rb=n//2
    a=pl.BlockSpec((1,rb,128),lambda i,me:(0,i,0))
    o=pl.BlockSpec((rb,768),lambda i,me:(0,0))
    return pl.pallas_call(outl_body,
        out_shape=(jax.ShapeDtypeStruct((rb,768),bf16),)*2,
        grid_spec=pltpu.PrefetchScalarGridSpec(num_scalar_prefetch=1,grid=(2,),
            in_specs=[a]*6+[pl.BlockSpec((w.shape[0],768),lambda i,me:(0,1),pipeline_mode=pl.Buffered(1)) for w in qb]+
              [pl.BlockSpec((rb,768),lambda i,me:(i,0))],
            out_specs=(o,o),
            scratch_shapes=[pltpu.VMEM((768,768),bf16)]),
        name="layer_output",
        cost_estimate=pl.CostEstimate(flops=2*n*768*768,transcendentals=0,bytes_accessed=n*768*8+768*768*2),
    )(me,*keep,*recv,*qb,mid)

def back_body(me, *refs, r_of):
    ka,ra=refs[:3],refs[3:6]
    u,t,low=refs[6:9]
    qa,qb=refs[9:13],refs[13:17]
    vec,eb,sums_two,keepA,sendA,keepB,sendB,ig_mine,ig_other,ws,b1T,acc,gs,os,ex=refs[17:]
    g=pl.program_id(0)
    gc=me[1]^g
    n=t.shape[0]
    @pl.when(g==0)
    def _():
        for i in range(4):
            rows=rows_of(me,i,qa[i].shape[0])
            for h in range(2):
                for j in range(2): ws[h,rows,j*384:(j+1)*384]=qa[i][:,(2*j+h)*384:(2*j+h+1)*384]
                ws[h,rows,768:1152]=qb[i][:,h*384:(h+1)*384]
        acc[...]=jnp.zeros_like(acc)
        ex[...]=jnp.zeros_like(ex)
        ex[4:5,:]=jnp.sum(u[...].astype(f32),axis=0,keepdims=True)
        ex[2:4,:]=sums_two[0:2,:]
        normed,_=norm_of(t[...])
        b1T[...]=(normed*vec[0:1,:]+vec[1:2,:]).astype(bf16).T
    def one(a):
        p=jnp.concatenate([r[j] for j in (1,2,3) for r in a],1)
        acc[...]+=dot_nt(p,ws[gc])
        gs[...]=dot(b1T[...],p).astype(bf16)
        os[pl.ds(pl.multiple_of(gc*384,384),384),:]=dot_tn(jnp.concatenate([r[0] for r in a],1),u[...]).astype(bf16)
        s=jnp.sum(p.astype(f32),axis=0,keepdims=True)
        for h in range(2):
            @pl.when(gc==h)
            def _():
                for j in range(3): ex[5+j:6+j,h*384:(h+1)*384]=s[:,j*384:(j+1)*384]
    @pl.when(g==0)
    def _(): one(ka)
    @pl.when(g==1)
    def _(): one(ra)
    for h in range(2):
        @pl.when(gc==h)
        def _():
            for i in range(4):
                A,B=((keepA,keepB),(sendA,sendB))[i%2]
                r=gs[rows_of(me,i,192),:]
                for j in range(2): A[i//2,:,(2*j+h)*384:(2*j+h+1)*384]=r[:,j*384:(j+1)*384]
                B[i//2,:,h*384:(h+1)*384]=r[:,768:]
    @pl.when(g==1)
    def _():
        normed,inv=norm_of(t[...])
        b=acc[...]
        ex[0:1,:]=jnp.sum(b*normed,axis=0,keepdims=True)
        ex[1:2,:]=jnp.sum(b,axis=0,keepdims=True)
        v=(low[...]+norm_back(b,normed,inv,vec[0:1,:])).astype(bf16)
        for h in range(2):
            @pl.when(me[0]==h)
            def _():
                ig_mine[...]=v[h*(n//2):(h+1)*(n//2)]
                ig_other[...]=v[(1-h)*(n//2):(2-h)*(n//2)]
        acc[0:768,0:EXTRA]=ex[...].T
        per=4*r_of
        for d in range(3072//per):
            q,o=divmod(d*per,768)
            acc[d*r_of:d*r_of+1,BIAS:BIAS+per]=eb[q,:,o:o+per]
        for i in range(4):
            A,B=((keepA,keepB),(sendA,sendB))[i%2]
            rows=rows_of(me,i,192)
            B[i//2,:,768:]=os[rows,:]
            A[i//2,:,1536:]=acc[rows,0:EXTRA].astype(bf16)

def back(me,keep,recv,u,t,low,qa,qb,vec,eb,sums_two,r):
    n=t.shape[0]
    S=jax.ShapeDtypeStruct; V=pltpu.VMEM
    A,B=(2,192,1536+EXTRA),(2,192,1536)
    return pl.pallas_call(functools.partial(back_body,r_of=r),
        out_shape=(S(A,bf16),S(A,bf16),S(B,bf16),S(B,bf16),S((n//2,768),bf16),S((n//2,768),bf16)),
        grid_spec=pltpu.PrefetchScalarGridSpec(num_scalar_prefetch=1,grid=(2,),
            in_specs=[WHOLE((4,n,128))]*6+[WHOLE((n,768))]*3+
              [WHOLE(w.shape) for w in qa]+[WHOLE((w.shape[0],768)) for w in qb]+[WHOLE((16,768)),WHOLE((4,1,768)),WHOLE((8,768))],
            out_specs=[WHOLE(A),WHOLE(A),WHOLE(B),WHOLE(B),WHOLE((n//2,768)),WHOLE((n//2,768))],
            scratch_shapes=[V((2,768,1152),bf16),V((768,n),bf16),V((n,768),f32),V((768,1152),bf16),V((768,768),bf16),V((EXTRA,768),f32)]),
        compiler_params=pltpu.CompilerParams(vmem_limit_bytes=58<<20),
        name="back",
        cost_estimate=pl.CostEstimate(flops=2*n*768*768*7,transcendentals=n,bytes_accessed=n*768*24+768*3072*6),
    )(me,*keep,*recv,u,t,low,*qa,*qb,vec,eb,sums_two)

def feed_body(me, t,u,e0,e1,e2,e3,r0,r1,r2,r3,be,vec, keepR,sendR,keepE,sendE,eb,mid,low,sums, b2,b2T,we,wr,act,hg,am,ab,egs,rgs, *, rb):
    s=pl.program_id(0)
    n=t.shape[0]; fb=we.shape[1]
    @pl.when(s==0)
    def _():
        def one(i,_):
            rows=pl.ds(pl.multiple_of(i*rb,rb),rb)
            normed,_=norm_of(t[rows,:])
            b=(normed*vec[2:3,:]+vec[3:4,:]).astype(bf16)
            b2[rows,:]=b
            b2T[i]=b.T
            am[rows,:]=t[rows,:].astype(f32)+(vec[4:5,:]+vec[5:6,:])
            ab[rows,:]=jnp.zeros((rb,768),f32)
            return 0
        lax.fori_loop(0,n//rb,one,0)
    for i,e in enumerate((e0,e1,e2,e3)): we[rows_of(me,i,192),:]=e[...]
    for i,r in enumerate((r0,r1,r2,r3)):
        @pl.when(s==i)
        def _(): wr[...]=r[...]
    def one(i,bs):
        rows=pl.ds(pl.multiple_of(i*rb,rb),rb)
        h=dot(b2[rows,:],we[...])+be[0]
        ag=dot_nt(u[rows,:],wr[...])
        cdf=0.5+0.5*lax.erf(h*0.7071067811865476)
        a=(h*cdf).astype(bf16)
        d=(ag*(cdf+h*(0.3989422804014327*jnp.exp(h*h*-0.5)))).astype(bf16)
        act[rows,:]=a; hg[rows,:]=d
        am[rows,:]+=dot(act[rows,:],wr[...])
        ab[rows,:]+=dot_nt(hg[rows,:],we[...])
        return bs+jnp.sum(d.astype(f32).reshape(rb//8,8,fb),axis=0)
    bs=lax.fori_loop(0,n//rb,one,jnp.zeros((8,fb),f32))
    eb[0]=jnp.sum(bs,axis=0,keepdims=True)
    rgs[...]=dot_tn(act[...],u[...]).astype(bf16)
    x=dot(b2T[0],hg[0:rb,:])
    for i in range(1,n//rb): x=x+dot(b2T[i],hg[i*rb:(i+1)*rb,:])
    egs[...]=x.astype(bf16)
    @pl.when(s%2==0)
    def _(): keepR[0]=rgs[...]
    @pl.when(s%2==1)
    def _(): sendR[0]=rgs[...]
    for i in range(4): (keepE,sendE)[i%2][i//2]=egs[rows_of(me,i,192),:]
    @pl.when(s==3)
    def _():
        def fin(i,c):
            rows=pl.ds(pl.multiple_of(i*rb,rb),rb)
            mid[rows,:]=am[rows,:]
            normed,inv=norm_of(t[rows,:])
            b=ab[rows,:]
            low[rows,:]=u[rows,:].astype(f32)+norm_back(b,normed,inv,vec[2:3,:])
            return c[0]+jnp.sum(b*normed,axis=0,keepdims=True),c[1]+jnp.sum(b,axis=0,keepdims=True)
        z=jnp.zeros((1,768),f32)
        p,q=lax.fori_loop(0,n//rb,fin,(z,z))
        sums[...]=jnp.zeros_like(sums)
        sums[0:1,:]=p; sums[1:2,:]=q

def feed(me,t,u,eq,rq,be,vec,rb=512):
    n=t.shape[0]; fb=768
    S=jax.ShapeDtypeStruct; V=pltpu.VMEM
    def qa(s,me): return (me[0]^(s//2))*2+(me[1]^(s%2))
    R=pl.BlockSpec((1,768,768),lambda s,me:(s//2,0,0))
    E=pl.BlockSpec((2,192,fb),lambda s,me:(0,0,qa(s,me)))
    return pl.pallas_call(functools.partial(feed_body,rb=rb),
        out_shape=[S((2,768,768),bf16)]*2+[S((2,192,4*fb),bf16)]*2+[S((4,1,fb),f32),S((n,768),f32),S((n,768),f32),S((8,768),f32)],
        grid_spec=pltpu.PrefetchScalarGridSpec(num_scalar_prefetch=1,grid=(4,),
            in_specs=[WHOLE((n,768))]*2+[pl.BlockSpec((192,fb),lambda s,me:(0,qa(s,me)))]*4+[WHOLE((768,768))]*4+
              [pl.BlockSpec((1,1,fb),lambda s,me:(qa(s,me),0,0)),WHOLE((16,768))],
            out_specs=[R,R,E,E,pl.BlockSpec((1,1,fb),lambda s,me:(qa(s,me),0,0))]+[WHOLE((n,768))]*2+[WHOLE((8,768))],
            scratch_shapes=[V((n,768),bf16),V((n//rb,768,rb),bf16),V((768,fb),bf16),V((fb,768),bf16),V((n,fb),bf16),V((n,fb),bf16),
                            V((n,768),f32),V((n,768),f32),V((768,fb),bf16),V((fb,768),bf16)]),
        compiler_params=pltpu.CompilerParams(vmem_limit_bytes=60<<20),
        name="feed",
        cost_estimate=pl.CostEstimate(flops=6*2*n*768*4*fb,transcendentals=n*4*fb*2,bytes_accessed=n*768*20+768*fb*32),
    )(me,t,u,*eq,*rq,be,vec)

def finish_body(*refs):
    pieces,(packed,output,expand,reduce_,*vecs)=refs[:-11],refs[-11:]
    count=len(pieces)//2
    r=packed.shape[0]
    def total(ps,*at):
        s=ps[0][at].astype(f32)
        for p in ps[1:]: s=s+p[at].astype(f32)
        return s
    s=total(pieces[:count],Ellipsis)
    packed[:,:1536]=s[:,:1536]
    packed[:,1536:]=s[:,1536+EXTRA:2304+EXTRA]
    output[...]=s[:,2304+EXTRA:]
    v=s[:,1536:1536+EXTRA].T
    for i in range(5): vecs[i][...]=v[i,:]
    vecs[5][...]=v[5:8,:]
    vecs[6][...]=s[0:1,1536+BIAS:1536+BIAS+4*r][0,:]
    e=total(pieces[count:],0)
    for i in range(4): expand[:,i*768:(i+1)*768]=e[i*r:(i+1)*r,:]
    reduce_[...]=total(pieces[count:],1)

def finish(pieces,feed_pieces):
    r=pieces[0].shape[0]
    S=jax.ShapeDtypeStruct
    o=pl.pallas_call(finish_body,out_shape=[S((r,2304),f32),S((r,768),f32),S((r,3072),f32),S((4*r,768),f32)]+[S((r,),f32)]*5+
        [S((3,r),f32),S((4*r,),f32)],name="finish")(*pieces,*feed_pieces)
    return o[:4],o[4:9],o[9],o[10]


def swap(a, axis):
    return lax.ppermute(a, axis, [(0, 1), (1, 0)])


def shift(a, axis, size, step):
    return lax.ppermute(a, axis, [(i, (i + step) % size) for i in range(size)])


def pick(index, here, there):
    place = lax.broadcasted_iota(jnp.int32, (2,) + (1,) * here.ndim, 0)
    return jnp.where(place == index, here[None], there[None])


def after(value, *others):
    return lax.optimization_barrier((value,) + others)[0]


def gather_line(shard, m):
    z = lax.axis_index("z")
    pieces = [shard] + [shift(shard, "z", m, step) for step in range(1, m)]
    back = (z - lax.broadcasted_iota(jnp.int32, (m,) + (1,) * shard.ndim, 0)) % m
    line = pieces[0][None]
    for step in range(1, m):
        line = jnp.where(back == step, pieces[step][None], line)
    return line


def join(y, near, far):
    return jnp.moveaxis(pick(y, near, far), 0, 1).reshape((-1,) + near.shape[2:])


def halve(a, y, m):
    a = a.reshape(a.shape[:-2] + (m, 2, -1) + a.shape[-1:])
    mine = lax.dynamic_index_in_dim(a, y, a.ndim - 3, keepdims=False)
    other = lax.dynamic_index_in_dim(a, 1 - y, a.ndim - 3, keepdims=False)
    return add(mine, swap(other, "y"), bf16)


def wide(a):
    a = a.reshape(a.shape[:-1] + (4, -1))
    return jnp.moveaxis(a, -2, -3).reshape(a.shape[:-3] + (-1, a.shape[-1]))


def add(a, b, dtype):
    return (a.astype(f32) + b.astype(f32)).astype(dtype)


def line_pieces(line, m):
    z = lax.axis_index("z")
    pieces = [lax.dynamic_index_in_dim(line, (z + step) % m, 0, keepdims=False) for step in range(m)]
    return pieces[:1] + [shift(p, "z", m, step + 1) for step, p in enumerate(pieces[1:])]


def rotary(length):
    half = ROT // 2
    frequency = rope_base ** (-(jnp.arange(half, dtype=f32) * 2.0 / ROT))
    lane = jnp.arange(128, dtype=jnp.int32) % HD
    frequency = jnp.tile(frequency, 16)[None, :]
    fine = jnp.arange(64, dtype=jnp.int32).astype(f32)[:, None] * frequency
    coarse = jnp.arange(0, length, 64, dtype=jnp.int32).astype(f32)[:, None] * frequency
    cf, sf = jnp.cos(fine)[None], jnp.sin(fine)[None]
    cc, sc = jnp.cos(coarse)[:, None], jnp.sin(coarse)[:, None]
    co = (cc * cf - sc * sf).reshape(length, 128)
    si = (sc * cf + cc * sf).reshape(length, 128)
    return jnp.stack(
        [
            jnp.where(lane < ROT, co, 1.0),
            jnp.where(lane < half, -si, 0.0),
            jnp.where((lane >= half) & (lane < ROT), si, 0.0),
        ]
    )


def exchange(mine, other, x):
    return pick(x, mine, swap(other, "x"))


def shards(
    inputs,
    first_gain,
    first_shift,
    second_gain,
    second_shift,
    packed_weight,
    packed_bias,
    output_weight,
    output_bias,
    expand_weight,
    expand_bias,
    reduce_weight,
    reduce_bias,
    cotangent,
    *,
    m,
):
    x, c, y = (lax.axis_index(a) for a in "xcy")
    me = jnp.stack([x, c]).astype(jnp.int32)
    block, width = inputs.shape[1:]
    r = first_gain.shape[0]
    first = 2 * width + EXTRA
    other_tokens = swap(lax.dynamic_index_in_dim(inputs, 1 - x, 0, keepdims=False), "x")
    vectors = [first_gain, first_shift, second_gain, second_shift, output_bias, reduce_bias]
    shard = pack(packed_weight, output_weight, vectors, packed_bias, expand_bias)
    table = rotary(4 * block)
    line = gather_line(shard, m)
    pair_r = jnp.stack([reduce_weight, swap(reduce_weight, "x")])
    line_a, line_b = line[:, :, :first], line[:, :, first:]
    far_b = swap(line_b, "x")
    near_a = join(y, line_a, swap(line_a, "y"))
    near_b = join(y, line_b, swap(line_b, "y"))
    far_a = swap(after(near_a, table), "x")
    far_b = join(y, far_b, swap(far_b, "y"))
    qa = [near_a, swap(near_a, "c"), far_a, swap(far_a, "c")]
    qb = [near_b, swap(near_b, "c"), far_b, swap(far_b, "c")]

    line_e = gather_line(expand_weight, m)
    line_r = gather_line(pair_r, m)
    other_grads = swap(lax.dynamic_index_in_dim(cotangent, 1 - x, 0, keepdims=False), "x")
    side_r = swap(line_r, "y")
    near_e = join(y, line_e, swap(line_e, "y"))

    own, send, t, vec, be = project(me, inputs, other_tokens, qa, qb, table, r)
    got = swap(send, "c")
    gown, gsend, u = upstream_heads(after(me, own), cotangent, other_grads, qb)
    ggot = swap(gsend, "c")
    core = me[1:]
    operands = (own, got, gown, ggot, table)
    keep0, give0 = attention(core, *operands, 0)

    near_r, far_r = (join(y, line_r[:, i], side_r[:, i]) for i in range(2))
    far_e = swap(near_e, "x")
    eq = [near_e, swap(near_e, "c"), far_e, swap(far_e, "c")]
    rq = [near_r, swap(near_r, "c"), far_r, swap(far_r, "c")]
    keep_r, send_r, keep_e, send_e, eb, mid, low, sums_two = feed(me, after(t, keep0), u, eq, rq, be, vec)
    keep1, give1 = attention(after(core, mid), *operands, 1)
    sum_r = add(keep_r, swap(send_r, "c"), bf16)
    sum_e = add(keep_e, swap(send_e, "c"), bf16)
    keep2, give2 = attention(after(core, keep1, sum_r, sum_e), *operands, 2)
    sum_r = add(sum_r[0], swap(sum_r[1], "x"), bf16)
    sum_e = halve(sum_e, y, m)
    keep = [keep0, keep1, keep2]
    recv = [swap(give0, "c"), swap(give1, "c"), swap(give2, "c")]
    out_mine, out_other = layer_output(after(me, sum_r, sum_e, keep2), keep, recv, qb, mid)
    sum_r = halve(sum_r, y, m)
    sum_e = add(sum_e[0], swap(sum_e[1], "x"), bf16)
    feed_line = jnp.stack([wide(sum_e), sum_r], 1)
    keep_a, send_a, keep_b, send_b, grad_mine, grad_other = back(
        after(me, out_mine), keep, recv, u, t, low, qa, qb, vec, eb, sums_two, r
    )
    feed_pieces = line_pieces(feed_line, m)
    layer_out = exchange(out_mine, out_other, x)
    sum_a = add(keep_a, swap(send_a, "c"), bf16)
    sum_b = add(keep_b, swap(send_b, "c"), bf16)
    line_a = halve(add(sum_a[0], swap(sum_a[1], "x"), bf16), y, m)
    sum_b = halve(sum_b, y, m)
    line_b = add(sum_b[0], swap(sum_b[1], "x"), bf16)
    input_grad = exchange(grad_mine, after(grad_other, layer_out), x)
    line = jnp.concatenate([line_a, line_b], 2)
    mats, v, packed_vec, expand_vec = finish(line_pieces(line, m), feed_pieces)
    packed_grad, output_grad, expand_grad, reduce_grad = mats
    return (
        layer_out,
        input_grad,
        v[0],
        v[1],
        v[2],
        v[3],
        packed_grad,
        packed_vec,
        output_grad,
        v[4],
        expand_grad,
        expand_vec,
        reduce_grad,
        v[4],
    )


def solution(mesh):
    shard = mesh.shape["shard"]
    m = shard // 2
    fine = Mesh(mesh.devices.reshape(2, 2, m, 2), ("x", "c", "z", "y"))
    every = ("x", "c", "z", "y")
    tokens = P(("z", "y"), ("x", "c"), None)
    vec, mat = P(every), P(every, None)
    in_specs = (tokens, vec, vec, vec, vec, mat, P(None, every), mat, vec, mat, vec, mat, vec, tokens)
    out_specs = (tokens, tokens, vec, vec, vec, vec, mat, P(None, every), mat, vec, mat, vec, mat, vec)

    def body(*args):
        return shards(*args, m=m)

    return jax.shard_map(body, mesh=fine, in_specs=in_specs, out_specs=out_specs, check_vma=False)
```

```python
import functools
import jax, jax.numpy as jnp
from jax import lax
from jax.experimental import pallas as pl
from jax.experimental.pallas import tpu as pltpu
from jax.sharding import Mesh, PartitionSpec as P

HD=64
ROT=16
f32=jnp.float32; bf16=jnp.bfloat16

def dot(a,b): return jnp.dot(a,b,preferred_element_type=f32)

def turn(v,tab,back):
    sgn=-1.0 if back else 1.0
    return v*tab[0]+sgn*(pltpu.roll(v,120,1)*tab[1]+pltpu.roll(v,8,1)*tab[2])

def attn_body(c_ref, own, par, gown, gpar, tab, keep, send, qs, ks, gs, vs, qT, gT, kT, vT, es0, es1, eb, dss, mx0, mx1, oT, dqT, dk, dv, *, blk, length, ch):
    c=c_ref[0]
    nb=length//blk
    lane=lax.broadcasted_iota(jnp.int32,(1,128),1)
    first=lane<HD
    for j,(d,dT) in enumerate(((qs,qT),(ks,kT),(vs,vT),(gs,gT))):
        for h in range(nb//2):
            hr=slice(h*blk,(h+1)*blk)
            a,b=(own[j,hr,:],par[j,hr,:]) if j<3 else (gown[hr,:],gpar[hr,:])
            pa=pl.multiple_of((2*h+c)*blk,blk); pb=pl.multiple_of((2*h+1-c)*blk,blk)
            d[pl.ds(pa,blk),:]=a
            d[pl.ds(pb,blk),:]=b
            dT[2*h+c]=a.T
            dT[2*h+1-c]=b.T
    dk[...]=jnp.zeros_like(dk); dv[...]=jnp.zeros_like(dv)
    kk=HD**-0.5*1.4426950408889634
    zero64=jnp.zeros((HD,blk),bf16)
    nc=blk//ch

    def masked(x): return [jnp.concatenate([x[:HD],zero64],0),jnp.concatenate([zero64,x[HD:]],0)]
    def top(x): return jnp.max(x.reshape(x.shape[0]//8,8,blk),axis=0)

    def score_diag(i,qh,es,mx):
        coli=lax.broadcasted_iota(jnp.int32,(ch,blk),1)
        rowi=lax.broadcasted_iota(jnp.int32,(ch,blk),0)
        for a in range(nc):
            rows=pl.ds(pl.multiple_of(i*blk+a*ch,ch),ch)
            k=ks[rows,:]
            for h in range(2):
                s=jnp.where(rowi+a*ch<=coli,dot(k,qh[h]),-1e30)
                es[h,rows,:]=s
                mx[h]=jnp.maximum(mx[h],top(s))

    mx0[...]=jnp.full_like(mx0,-1e30)
    score_diag(0,masked(qT[0]),es0,mx0)

    def block(i,es,mx,es_next,mx_next):
        i1=jnp.minimum(i+1,nb-1)
        rows=pl.ds(pl.multiple_of(i*blk,blk),blk)
        q1=masked(qT[i1])
        mk=[jnp.max(mx[h],axis=0,keepdims=True)*kk for h in range(2)]
        mx_next[...]=jnp.full((2,8,blk),-1e30,f32)
        oT[...]=jnp.zeros_like(oT)
        def sB(j,l):
            out=list(l)
            for a in range(nc):
                kr=pl.ds(pl.multiple_of(j*blk+a*ch,ch),ch)
                k=ks[kr,:]
                for h in range(2):
                    s=dot(k,q1[h])
                    es_next[h,kr,:]=s
                    mx_next[h]=jnp.maximum(mx_next[h],top(s))
                    e=jnp.exp2(es[h,kr,:]*kk-mk[h])
                    es[h,kr,:]=e
                    eb[h,kr,:]=e.astype(bf16)
                    out[h]=out[h]+jnp.sum(e.reshape(ch//8,8,blk),axis=0)
            jr=pl.ds(pl.multiple_of(j*blk,blk),blk)
            for h in range(2):
                hs=slice(h*HD,(h+1)*HD)
                oT[hs,:]+=dot(vT[j,hs,:],eb[h,jr,:])
            return tuple(out)
        z=jnp.zeros((8,blk),f32)
        l=lax.fori_loop(0,i+1,sB,(z,z))
        @pl.when(i<nb-1)
        def _(): score_diag(i1,q1,es_next,mx_next)
        r=[1.0/jnp.sum(t,axis=0,keepdims=True) for t in l]
        gt=gT[i]
        sc=jnp.concatenate([(gt[h*HD:(h+1)*HD].astype(f32)*r[h]) for h in range(2)],0).astype(bf16)
        gh=masked(sc)
        o=[oT[h*HD:(h+1)*HD,:]*r[h] for h in range(2)]
        D=[jnp.sum(o[h]*sc[h*HD:(h+1)*HD].astype(f32),axis=0,keepdims=True) for h in range(2)]
        oT[...]=jnp.concatenate(o,0)
        g=sc.T
        q=qs[rows,:]
        zq=jnp.zeros_like(q)
        qm=[jnp.where(first,q,zq),jnp.where(first,zq,q)]
        gm=[jnp.where(first,g,zq),jnp.where(first,zq,g)]
        dqT[...]=jnp.zeros_like(dqT)
        def sC(j,_):
            for a in range(nc):
                kr=pl.ds(pl.multiple_of(j*blk+a*ch,ch),ch)
                v=vs[kr,:]
                ds=[(es[h,kr,:]*(dot(v,gh[h])-D[h])).astype(bf16) for h in range(2)]
                for h in range(2): dss[h,a*ch:(a+1)*ch,:]=ds[h]
                dv[kr,:]+=dot(eb[0,kr,:],gm[0])+dot(eb[1,kr,:],gm[1])
                dk[kr,:]+=dot(ds[0],qm[0])+dot(ds[1],qm[1])
            for h in range(2):
                hs=slice(h*HD,(h+1)*HD)
                dqT[hs,:]+=dot(kT[j,hs,:],dss[h])
            return 0
        lax.fori_loop(0,i+1,sC,0)
        qs[rows,:]=(dqT[...].T*HD**-0.5).astype(bf16)
        gs[rows,:]=oT[...].T.astype(bf16)

    def two(i,_):
        block(2*i,es0,mx0,es1,mx1)
        block(2*i+1,es1,mx1,es0,mx0)
        return 0
    lax.fori_loop(0,nb//2,two,0)
    for h in range(nb//2):
        for who,ref in ((c,keep),(1-c,send)):
            rows=pl.ds(pl.multiple_of((2*h+who)*blk,blk),blk)
            dst=slice(h*blk,(h+1)*blk)
            t=[tab[n,rows,:] for n in range(3)]
            ref[0,dst,:]=gs[rows,:]
            ref[1,dst,:]=turn(qs[rows,:].astype(f32),t,True).astype(bf16)
            ref[2,dst,:]=turn((dk[rows,:]*HD**-0.5).astype(bf16).astype(f32),t,True).astype(bf16)
            ref[3,dst,:]=dv[rows,:].astype(bf16)

def attention(c, own, par, gown, gpar, tab, pair, npair=1, blk=512, ch=512):
    rows=own.shape[1]; length=2*rows
    nb=length//blk
    spec=pl.BlockSpec((3,rows,128),lambda p,c:(0,0,p+pair))
    gspec=pl.BlockSpec((rows,128),lambda p,c:(0,p+pair))
    ospec=pl.BlockSpec((4,rows,128),lambda p,c:(0,0,p))
    V=pltpu.VMEM
    return pl.pallas_call(
        functools.partial(attn_body,blk=blk,length=length,ch=ch),
        out_shape=(jax.ShapeDtypeStruct((4,rows,128*npair),bf16),)*2,
        grid_spec=pltpu.PrefetchScalarGridSpec(num_scalar_prefetch=1,grid=(npair,),
            in_specs=[spec,spec,gspec,gspec,pl.BlockSpec((3,length,128),lambda p,c:(0,0,0),pipeline_mode=pl.Buffered(1))],
            out_specs=[ospec,ospec],
            scratch_shapes=[V((length,128),bf16)]*4+[V((nb,128,blk),bf16)]*4+
              [V((2,length,blk),f32),V((2,length,blk),f32),V((2,length,blk),bf16),V((2,blk,blk),bf16),V((2,8,blk),f32),V((2,8,blk),f32),
               V((128,blk),f32),V((128,blk),f32),V((length,128),f32),V((length,128),f32)]),
        compiler_params=pltpu.CompilerParams(vmem_limit_bytes=58<<20),
        name="attention",
        cost_estimate=pl.CostEstimate(flops=int(6*2*length*length//2*HD*2*npair*4),transcendentals=length*length*npair,bytes_accessed=16*rows*128*2*npair),
    )(c,own,par,gown,gpar,tab)
eps_norm = 1e-05
rope_base = 10000.0
EXTRA = 128
BIAS = 32

def dot_nt(a,b): return lax.dot_general(a,b,(((1,),(1,)),((),())),preferred_element_type=f32)
def dot_tn(a,b): return lax.dot_general(a,b,(((0,),(0,)),((),())),preferred_element_type=f32)

def norm_of(x):
    x=x.astype(f32)
    ce=x-jnp.mean(x,axis=-1,keepdims=True)
    inv=lax.rsqrt(jnp.mean(ce*ce,axis=-1,keepdims=True)+eps_norm)
    return ce*inv,inv

def norm_back(up,normed,inv,gain):
    s=up*gain
    return inv*(s-jnp.mean(s,axis=-1,keepdims=True)-normed*jnp.mean(s*normed,axis=-1,keepdims=True))

WHOLE=lambda shape: pl.BlockSpec(shape,lambda *a:(0,)*len(shape),pipeline_mode=pl.Buffered(1))

def pack_body(pk,ow,a,b,c,d,e,f,pb,eb,out,s):
    r=out.shape[0]
    s[...]=jnp.zeros_like(s)
    for k,v in enumerate((a,b,c,d,e,f)): s[k:k+1,0:r]=v[...].astype(f32)[None,:]
    s[6:9,0:r]=pb[...].astype(f32)
    out[:,:1536]=pk[:,:1536]
    s[...]=s[...].T
    s[0:1,BIAS:BIAS+4*r]=eb[...].astype(f32)[None,:]
    out[:,1536:1536+EXTRA]=s[0:r,:].astype(bf16)
    out[:,1536+EXTRA:2304+EXTRA]=pk[:,1536:]
    out[:,2304+EXTRA:]=ow[...]
def pack(pk,ow,vecs,pb,eb):
    return pl.pallas_call(pack_body,out_shape=jax.ShapeDtypeStruct((pk.shape[0],3072+EXTRA),bf16),
        scratch_shapes=[pltpu.VMEM((EXTRA,128),f32)],name="pack")(pk,ow,*vecs,pb,eb)

def quarter(me_ref,n):
    return (me_ref[0]^(n//2))*2+(me_ref[1]^(n%2))

def rows_of(me_ref,n,q):
    return pl.ds(pl.multiple_of(quarter(me_ref,n)*q,q),q)

def split(c,value,keep,send,half):
    for k in range(2):
        @pl.when(c==k)
        def _():
            keep[...]=value[:,k*half:(k+1)*half]
            send[...]=value[:,(1-k)*half:(2-k)*half]

def proj_body(me, a, b, *refs, r_of):
    qa,qb=refs[:4],refs[4:8]
    tab,keep,send,t,vec,be,ws,ex,st=refs[8:]
    i=pl.program_id(0)
    @pl.when(i==0)
    def _():
        for n in range(4):
            rows=rows_of(me,n,qa[n].shape[0])
            ws[rows,:1536]=qa[n][:,:1536]
            ws[rows,1536:]=qb[n][...]
            ex[rows,:]=qa[n][:,1536:].astype(f32)
        vec[...]=ex[...].T[:16,:]
        per=4*r_of
        for d in range(3072//per):
            q,o=divmod(d*per,768)
            be[q,:,o:o+per]=ex[d*r_of:d*r_of+1,BIAS:BIAS+per]
    x=jnp.where(i==me[0],a[0],b[...])
    t[...]=x
    normed,_=norm_of(x)
    b1=(normed*vec[0:1,:]+vec[1:2,:]).astype(bf16)
    half=x.shape[0]//2
    rows=[slice(r*half,(r+1)*half) for r in range(2)]
    vs=[[dot(b1[r,:],ws[:,j*768:(j+1)*768])+vec[6+j:7+j,:] for r in rows] for j in range(3)]
    for r in range(2):
        tb=[tab[n,rows[r],:] for n in range(3)]
        for j in range(2):
            for g in range(6): st[j,rows[r],g*128:(g+1)*128]=turn(vs[j][r][:,g*128:(g+1)*128],tb,False).astype(bf16)
        st[2,rows[r],:]=vs[2][r].astype(bf16)
    for k in range(2):
        @pl.when(me[1]==k)
        def _():
            keep[...]=st[:,:,k*384:(k+1)*384]
            send[...]=st[:,:,(1-k)*384:(2-k)*384]

def project(me,mine,other,qa,qb,tab,r):
    n=2*other.shape[0]; rb=n//2; per=1
    S=jax.ShapeDtypeStruct
    out=pl.BlockSpec((3,rb,384),lambda i,me:(0,i,0))
    return pl.pallas_call(functools.partial(proj_body,r_of=r),
        out_shape=(S((3,n,384),bf16),S((3,n,384),bf16),S((n,768),bf16),S((16,768),f32),S((4,1,768),f32)),
        grid_spec=pltpu.PrefetchScalarGridSpec(num_scalar_prefetch=1,grid=(n//rb,),
            in_specs=[pl.BlockSpec((1,rb,768),lambda i,me:(me[0],i%per,0)),pl.BlockSpec((rb,768),lambda i,me:(i%per,0))]+
              [WHOLE(w.shape) for w in qa]+[WHOLE((w.shape[0],768)) for w in qb]+
              [pl.BlockSpec((3,rb,128),lambda i,me:(0,(2*(i//per)+me[1])*per+i%per,0))],
            out_specs=(out,out,pl.BlockSpec((rb,768),lambda i,me:(i,0)),pl.BlockSpec((16,768),lambda i,me:(0,0)),pl.BlockSpec((4,1,768),lambda i,me:(0,0,0))),
            scratch_shapes=[pltpu.VMEM((768,2304),bf16),pltpu.VMEM((768,EXTRA),f32),pltpu.VMEM((3,rb,768),bf16)]),
        compiler_params=pltpu.CompilerParams(vmem_limit_bytes=56<<20),
        name="project",
        cost_estimate=pl.CostEstimate(flops=2*n*768*2304,transcendentals=n,bytes_accessed=n*768*10+768*3072*2),
    )(me,mine,other,*qa,*qb,tab)

def upst_body(me, a, b, *refs):
    qb,(keep,send,u,ws)=refs[:4],refs[4:]
    i=pl.program_id(0)
    @pl.when(i==0)
    def _():
        for n in range(4): ws[rows_of(me,n,qb[n].shape[0]),:]=qb[n][...]
    x=jnp.where(i==me[0],a[0],b[...])
    u[...]=x
    half=x.shape[0]//2
    split(me[1],jnp.concatenate([dot_nt(x[:half],ws[...]),dot_nt(x[half:],ws[...])],0).astype(bf16),keep,send,384)

def upstream_heads(me,mine,other,qb):
    n=2*other.shape[0]; rb=n//2; per=1
    S=jax.ShapeDtypeStruct
    out=pl.BlockSpec((rb,384),lambda i,me:(i,0))
    return pl.pallas_call(upst_body,
        out_shape=(S((n,384),bf16),S((n,384),bf16),S((n,768),bf16)),
        grid_spec=pltpu.PrefetchScalarGridSpec(num_scalar_prefetch=1,grid=(n//rb,),
            in_specs=[pl.BlockSpec((1,rb,768),lambda i,me:(me[0],i%per,0)),pl.BlockSpec((rb,768),lambda i,me:(i%per,0))]+
              [pl.BlockSpec((w.shape[0],768),lambda i,me:(0,1),pipeline_mode=pl.Buffered(1)) for w in qb],
            out_specs=(out,out,pl.BlockSpec((rb,768),lambda i,me:(i,0))),
            scratch_shapes=[pltpu.VMEM((768,768),bf16)]),
        name="upstream",
        cost_estimate=pl.CostEstimate(flops=2*n*768*768,transcendentals=0,bytes_accessed=n*768*6+768*768*2),
    )(me,mine,other,*qb)

def outl_body(me, *refs):
    ka,ra,qb=refs[:3],refs[3:6],refs[6:10]
    mid,mine,other,wos=refs[10:]
    i=pl.program_id(0)
    @pl.when(i==0)
    def _():
        for n in range(4): wos[rows_of(me,n,qb[n].shape[0]),:]=qb[n][...]
    half=mid.shape[0]//2
    outs=[]
    for r in (slice(0,half),slice(half,2*half)):
        acc=mid[r,:]
        for g,a in ((0,ka),(1,ra)):
            rows=pl.ds(pl.multiple_of((me[1]^g)*384,384),384)
            acc=acc+dot(jnp.concatenate([p[0,r,:] for p in a],1),wos[rows,:])
        outs.append(acc.astype(bf16))
    out=jnp.concatenate(outs,0)
    @pl.when(i==me[0])
    def _(): mine[...]=out
    @pl.when(i!=me[0])
    def _(): other[...]=out

def layer_output(me,keep,recv,qb,mid):
    n=mid.shape[0]; rb=n//2
    a=pl.BlockSpec((1,rb,128),lambda i,me:(0,i,0))
    o=pl.BlockSpec((rb,768),lambda i,me:(0,0))
    return pl.pallas_call(outl_body,
        out_shape=(jax.ShapeDtypeStruct((rb,768),bf16),)*2,
        grid_spec=pltpu.PrefetchScalarGridSpec(num_scalar_prefetch=1,grid=(2,),
            in_specs=[a]*6+[pl.BlockSpec((w.shape[0],768),lambda i,me:(0,1),pipeline_mode=pl.Buffered(1)) for w in qb]+
              [pl.BlockSpec((rb,768),lambda i,me:(i,0))],
            out_specs=(o,o),
            scratch_shapes=[pltpu.VMEM((768,768),bf16)]),
        name="layer_output",
        cost_estimate=pl.CostEstimate(flops=2*n*768*768,transcendentals=0,bytes_accessed=n*768*8+768*768*2),
    )(me,*keep,*recv,*qb,mid)

def back_body(me, *refs, r_of):
    ka,ra=refs[:3],refs[3:6]
    u,t,low=refs[6:9]
    qa,qb=refs[9:13],refs[13:17]
    vec,eb,sums_two,keepA,sendA,keepB,sendB,ig_mine,ig_other,ws,b1T,acc,gs,os,ex=refs[17:]
    g=pl.program_id(0)
    gc=me[1]^g
    n=t.shape[0]
    @pl.when(g==0)
    def _():
        for i in range(4):
            rows=rows_of(me,i,qa[i].shape[0])
            for h in range(2):
                for j in range(2): ws[h,rows,j*384:(j+1)*384]=qa[i][:,(2*j+h)*384:(2*j+h+1)*384]
                ws[h,rows,768:1152]=qb[i][:,h*384:(h+1)*384]
        acc[...]=jnp.zeros_like(acc)
        ex[...]=jnp.zeros_like(ex)
        ex[4:5,:]=jnp.sum(u[...].astype(f32),axis=0,keepdims=True)
        ex[2:4,:]=sums_two[0:2,:]
        normed,_=norm_of(t[...])
        b1T[...]=(normed*vec[0:1,:]+vec[1:2,:]).astype(bf16).T
    def one(a):
        p=jnp.concatenate([r[j] for j in (1,2,3) for r in a],1)
        acc[...]+=dot_nt(p,ws[gc])
        gs[...]=dot(b1T[...],p).astype(bf16)
        os[pl.ds(pl.multiple_of(gc*384,384),384),:]=dot_tn(jnp.concatenate([r[0] for r in a],1),u[...]).astype(bf16)
        s=jnp.sum(p.astype(f32),axis=0,keepdims=True)
        for h in range(2):
            @pl.when(gc==h)
            def _():
                for j in range(3): ex[5+j:6+j,h*384:(h+1)*384]=s[:,j*384:(j+1)*384]
    @pl.when(g==0)
    def _(): one(ka)
    @pl.when(g==1)
    def _(): one(ra)
    for h in range(2):
        @pl.when(gc==h)
        def _():
            for i in range(4):
                A,B=((keepA,keepB),(sendA,sendB))[i%2]
                r=gs[rows_of(me,i,192),:]
                for j in range(2): A[i//2,:,(2*j+h)*384:(2*j+h+1)*384]=r[:,j*384:(j+1)*384]
                B[i//2,:,h*384:(h+1)*384]=r[:,768:]
    @pl.when(g==1)
    def _():
        normed,inv=norm_of(t[...])
        b=acc[...]
        ex[0:1,:]=jnp.sum(b*normed,axis=0,keepdims=True)
        ex[1:2,:]=jnp.sum(b,axis=0,keepdims=True)
        v=(low[...]+norm_back(b,normed,inv,vec[0:1,:])).astype(bf16)
        for h in range(2):
            @pl.when(me[0]==h)
            def _():
                ig_mine[...]=v[h*(n//2):(h+1)*(n//2)]
                ig_other[...]=v[(1-h)*(n//2):(2-h)*(n//2)]
        acc[0:768,0:EXTRA]=ex[...].T
        per=4*r_of
        for d in range(3072//per):
            q,o=divmod(d*per,768)
            acc[d*r_of:d*r_of+1,BIAS:BIAS+per]=eb[q,:,o:o+per]
        for i in range(4):
            A,B=((keepA,keepB),(sendA,sendB))[i%2]
            rows=rows_of(me,i,192)
            B[i//2,:,768:]=os[rows,:]
            A[i//2,:,1536:]=acc[rows,0:EXTRA].astype(bf16)

def back(me,keep,recv,u,t,low,qa,qb,vec,eb,sums_two,r):
    n=t.shape[0]
    S=jax.ShapeDtypeStruct; V=pltpu.VMEM
    A,B=(2,192,1536+EXTRA),(2,192,1536)
    return pl.pallas_call(functools.partial(back_body,r_of=r),
        out_shape=(S(A,bf16),S(A,bf16),S(B,bf16),S(B,bf16),S((n//2,768),bf16),S((n//2,768),bf16)),
        grid_spec=pltpu.PrefetchScalarGridSpec(num_scalar_prefetch=1,grid=(2,),
            in_specs=[WHOLE((4,n,128))]*6+[WHOLE((n,768))]*3+
              [WHOLE(w.shape) for w in qa]+[WHOLE((w.shape[0],768)) for w in qb]+[WHOLE((16,768)),WHOLE((4,1,768)),WHOLE((8,768))],
            out_specs=[WHOLE(A),WHOLE(A),WHOLE(B),WHOLE(B),WHOLE((n//2,768)),WHOLE((n//2,768))],
            scratch_shapes=[V((2,768,1152),bf16),V((768,n),bf16),V((n,768),f32),V((768,1152),bf16),V((768,768),bf16),V((EXTRA,768),f32)]),
        compiler_params=pltpu.CompilerParams(vmem_limit_bytes=58<<20),
        name="back",
        cost_estimate=pl.CostEstimate(flops=2*n*768*768*7,transcendentals=n,bytes_accessed=n*768*24+768*3072*6),
    )(me,*keep,*recv,u,t,low,*qa,*qb,vec,eb,sums_two)

def feed_body(me, t,u,e0,e1,e2,e3,r0,r1,r2,r3,be,vec, keepR,sendR,keepE,sendE,eb,mid,low,sums, b2,b2T,we,wr,act,hg,am,ab,egs,rgs, *, rb):
    s=pl.program_id(0)
    n=t.shape[0]; fb=we.shape[1]
    @pl.when(s==0)
    def _():
        def one(i,_):
            rows=pl.ds(pl.multiple_of(i*rb,rb),rb)
            normed,_=norm_of(t[rows,:])
            b=(normed*vec[2:3,:]+vec[3:4,:]).astype(bf16)
            b2[rows,:]=b
            b2T[i]=b.T
            am[rows,:]=t[rows,:].astype(f32)+(vec[4:5,:]+vec[5:6,:])
            ab[rows,:]=jnp.zeros((rb,768),f32)
            return 0
        lax.fori_loop(0,n//rb,one,0)
    for i,e in enumerate((e0,e1,e2,e3)): we[rows_of(me,i,192),:]=e[...]
    for i,r in enumerate((r0,r1,r2,r3)):
        @pl.when(s==i)
        def _(): wr[...]=r[...]
    def one(i,bs):
        rows=pl.ds(pl.multiple_of(i*rb,rb),rb)
        h=dot(b2[rows,:],we[...])+be[0]
        ag=dot_nt(u[rows,:],wr[...])
        cdf=0.5+0.5*lax.erf(h*0.7071067811865476)
        a=(h*cdf).astype(bf16)
        d=(ag*(cdf+h*(0.3989422804014327*jnp.exp(h*h*-0.5)))).astype(bf16)
        act[rows,:]=a; hg[rows,:]=d
        am[rows,:]+=dot(act[rows,:],wr[...])
        ab[rows,:]+=dot_nt(hg[rows,:],we[...])
        return bs+jnp.sum(d.astype(f32).reshape(rb//8,8,fb),axis=0)
    bs=lax.fori_loop(0,n//rb,one,jnp.zeros((8,fb),f32))
    eb[0]=jnp.sum(bs,axis=0,keepdims=True)
    rgs[...]=dot_tn(act[...],u[...]).astype(bf16)
    x=dot(b2T[0],hg[0:rb,:])
    for i in range(1,n//rb): x=x+dot(b2T[i],hg[i*rb:(i+1)*rb,:])
    egs[...]=x.astype(bf16)
    @pl.when(s%2==0)
    def _(): keepR[0]=rgs[...]
    @pl.when(s%2==1)
    def _(): sendR[0]=rgs[...]
    for i in range(4): (keepE,sendE)[i%2][i//2]=egs[rows_of(me,i,192),:]
    @pl.when(s==3)
    def _():
        def fin(i,c):
            rows=pl.ds(pl.multiple_of(i*rb,rb),rb)
            mid[rows,:]=am[rows,:]
            normed,inv=norm_of(t[rows,:])
            b=ab[rows,:]
            low[rows,:]=u[rows,:].astype(f32)+norm_back(b,normed,inv,vec[2:3,:])
            return c[0]+jnp.sum(b*normed,axis=0,keepdims=True),c[1]+jnp.sum(b,axis=0,keepdims=True)
        z=jnp.zeros((1,768),f32)
        p,q=lax.fori_loop(0,n//rb,fin,(z,z))
        sums[...]=jnp.zeros_like(sums)
        sums[0:1,:]=p; sums[1:2,:]=q

def feed(me,t,u,eq,rq,be,vec,rb=512):
    n=t.shape[0]; fb=768
    S=jax.ShapeDtypeStruct; V=pltpu.VMEM
    def qa(s,me): return (me[0]^(s//2))*2+(me[1]^(s%2))
    R=pl.BlockSpec((1,768,768),lambda s,me:(s//2,0,0))
    E=pl.BlockSpec((2,192,fb),lambda s,me:(0,0,qa(s,me)))
    return pl.pallas_call(functools.partial(feed_body,rb=rb),
        out_shape=[S((2,768,768),bf16)]*2+[S((2,192,4*fb),bf16)]*2+[S((4,1,fb),f32),S((n,768),f32),S((n,768),f32),S((8,768),f32)],
        grid_spec=pltpu.PrefetchScalarGridSpec(num_scalar_prefetch=1,grid=(4,),
            in_specs=[WHOLE((n,768))]*2+[pl.BlockSpec((192,fb),lambda s,me:(0,qa(s,me)))]*4+[WHOLE((768,768))]*4+
              [pl.BlockSpec((1,1,fb),lambda s,me:(qa(s,me),0,0)),WHOLE((16,768))],
            out_specs=[R,R,E,E,pl.BlockSpec((1,1,fb),lambda s,me:(qa(s,me),0,0))]+[WHOLE((n,768))]*2+[WHOLE((8,768))],
            scratch_shapes=[V((n,768),bf16),V((n//rb,768,rb),bf16),V((768,fb),bf16),V((fb,768),bf16),V((n,fb),bf16),V((n,fb),bf16),
                            V((n,768),f32),V((n,768),f32),V((768,fb),bf16),V((fb,768),bf16)]),
        compiler_params=pltpu.CompilerParams(vmem_limit_bytes=60<<20),
        name="feed",
        cost_estimate=pl.CostEstimate(flops=6*2*n*768*4*fb,transcendentals=n*4*fb*2,bytes_accessed=n*768*20+768*fb*32),
    )(me,t,u,*eq,*rq,be,vec)

def finish_body(*refs):
    pieces,(packed,output,expand,reduce_,*vecs)=refs[:-11],refs[-11:]
    count=len(pieces)//2
    r=packed.shape[0]
    def total(ps,*at):
        s=ps[0][at].astype(f32)
        for p in ps[1:]: s=s+p[at].astype(f32)
        return s
    s=total(pieces[:count],Ellipsis)
    packed[:,:1536]=s[:,:1536]
    packed[:,1536:]=s[:,1536+EXTRA:2304+EXTRA]
    output[...]=s[:,2304+EXTRA:]
    v=s[:,1536:1536+EXTRA].T
    for i in range(5): vecs[i][...]=v[i,:]
    vecs[5][...]=v[5:8,:]
    vecs[6][...]=s[0:1,1536+BIAS:1536+BIAS+4*r][0,:]
    e=total(pieces[count:],0)
    for i in range(4): expand[:,i*768:(i+1)*768]=e[i*r:(i+1)*r,:]
    reduce_[...]=total(pieces[count:],1)

def finish(pieces,feed_pieces):
    r=pieces[0].shape[0]
    S=jax.ShapeDtypeStruct
    o=pl.pallas_call(finish_body,out_shape=[S((r,2304),f32),S((r,768),f32),S((r,3072),f32),S((4*r,768),f32)]+[S((r,),f32)]*5+
        [S((3,r),f32),S((4*r,),f32)],name="finish")(*pieces,*feed_pieces)
    return o[:4],o[4:9],o[9],o[10]


def swap(a, axis):
    return lax.ppermute(a, axis, [(0, 1), (1, 0)])


def shift(a, axis, size, step):
    return lax.ppermute(a, axis, [(i, (i + step) % size) for i in range(size)])


def pick(index, here, there):
    place = lax.broadcasted_iota(jnp.int32, (2,) + (1,) * here.ndim, 0)
    return jnp.where(place == index, here[None], there[None])


def after(value, *others):
    return lax.optimization_barrier((value,) + others)[0]


def gather_line(shard, m):
    z = lax.axis_index("z")
    pieces = [shard] + [shift(shard, "z", m, step) for step in range(1, m)]
    back = (z - lax.broadcasted_iota(jnp.int32, (m,) + (1,) * shard.ndim, 0)) % m
    line = pieces[0][None]
    for step in range(1, m):
        line = jnp.where(back == step, pieces[step][None], line)
    return line


def join(y, near, far):
    return jnp.moveaxis(pick(y, near, far), 0, 1).reshape((-1,) + near.shape[2:])


def add3(a, b, c):
    return (a.astype(f32) + b.astype(f32) + c.astype(f32)).astype(bf16)


def part(a, y, m):
    a = a.reshape(a.shape[:-2] + (m, 2, -1) + a.shape[-1:])
    return lax.dynamic_index_in_dim(a, y, a.ndim - 3, keepdims=False)


def halve(a, y, m):
    return add(part(a, y, m), swap(part(a, 1 - y, m), "y"), bf16)


def wide(a):
    a = a.reshape(a.shape[:-1] + (4, -1))
    return jnp.moveaxis(a, -2, -3).reshape(a.shape[:-3] + (-1, a.shape[-1]))


def add(a, b, dtype):
    return (a.astype(f32) + b.astype(f32)).astype(dtype)


def line_pieces(line, m):
    z = lax.axis_index("z")
    pieces = [lax.dynamic_index_in_dim(line, (z + step) % m, 0, keepdims=False) for step in range(m)]
    return pieces[:1] + [shift(p, "z", m, step + 1) for step, p in enumerate(pieces[1:])]


def rotary(length):
    half = ROT // 2
    frequency = rope_base ** (-(jnp.arange(half, dtype=f32) * 2.0 / ROT))
    lane = jnp.arange(128, dtype=jnp.int32) % HD
    frequency = jnp.tile(frequency, 16)[None, :]
    fine = jnp.arange(64, dtype=jnp.int32).astype(f32)[:, None] * frequency
    coarse = jnp.arange(0, length, 64, dtype=jnp.int32).astype(f32)[:, None] * frequency
    cf, sf = jnp.cos(fine)[None], jnp.sin(fine)[None]
    cc, sc = jnp.cos(coarse)[:, None], jnp.sin(coarse)[:, None]
    co = (cc * cf - sc * sf).reshape(length, 128)
    si = (sc * cf + cc * sf).reshape(length, 128)
    return jnp.stack(
        [
            jnp.where(lane < ROT, co, 1.0),
            jnp.where(lane < half, -si, 0.0),
            jnp.where((lane >= half) & (lane < ROT), si, 0.0),
        ]
    )


def exchange(mine, other, x):
    return pick(x, mine, swap(other, "x"))


def shards(
    inputs,
    first_gain,
    first_shift,
    second_gain,
    second_shift,
    packed_weight,
    packed_bias,
    output_weight,
    output_bias,
    expand_weight,
    expand_bias,
    reduce_weight,
    reduce_bias,
    cotangent,
    *,
    m,
):
    x, c, y = (lax.axis_index(a) for a in "xcy")
    me = jnp.stack([x, c]).astype(jnp.int32)
    block, width = inputs.shape[1:]
    r = first_gain.shape[0]
    first = 2 * width + EXTRA
    other_tokens = swap(lax.dynamic_index_in_dim(inputs, 1 - x, 0, keepdims=False), "x")
    vectors = [first_gain, first_shift, second_gain, second_shift, output_bias, reduce_bias]
    shard = pack(packed_weight, output_weight, vectors, packed_bias, expand_bias)
    table = rotary(4 * block)
    line = gather_line(shard, m)
    pair_r = jnp.stack([reduce_weight, swap(reduce_weight, "x")])
    line_a, line_b = line[:, :, :first], line[:, :, first:]
    far_b = swap(line_b, "x")
    near_a = join(y, line_a, swap(line_a, "y"))
    near_b = join(y, line_b, swap(line_b, "y"))
    far_a = swap(after(near_a, table), "x")
    far_b = join(y, far_b, swap(far_b, "y"))
    qa = [near_a, swap(near_a, "c"), far_a, swap(far_a, "c")]
    qb = [near_b, swap(near_b, "c"), far_b, swap(far_b, "c")]

    line_e = gather_line(expand_weight, m)
    line_r = gather_line(pair_r, m)
    other_grads = swap(lax.dynamic_index_in_dim(cotangent, 1 - x, 0, keepdims=False), "x")
    side_r = swap(line_r, "y")
    near_e = join(y, line_e, swap(line_e, "y"))

    own, send, t, vec, be = project(me, inputs, other_tokens, qa, qb, table, r)
    got = swap(send, "c")
    gown, gsend, u = upstream_heads(after(me, own), cotangent, other_grads, qb)
    ggot = swap(gsend, "c")
    core = me[1:]
    operands = (own, got, gown, ggot, table)
    keep0, give0 = attention(core, *operands, 0)

    near_r, far_r = (join(y, line_r[:, i], side_r[:, i]) for i in range(2))
    far_e = swap(near_e, "x")
    eq = [near_e, swap(near_e, "c"), far_e, swap(far_e, "c")]
    rq = [near_r, swap(near_r, "c"), far_r, swap(far_r, "c")]
    keep_r, send_r, keep_e, send_e, eb, mid, low, sums_two = feed(me, after(t, keep0), u, eq, rq, be, vec)
    keep1, give1 = attention(after(core, mid), *operands, 1)
    got_r, got_e = swap(send_r, "c"), swap(send_e, "c")
    far_r = add(keep_r[1], got_r[1], bf16)
    far_e = add(part(keep_e, 1 - y, m), part(got_e, 1 - y, m), bf16)
    keep2, give2 = attention(after(core, keep1, far_r, far_e), *operands, 2)
    sum_r = add3(keep_r[0], got_r[0], swap(far_r, "x"))
    sum_e = add3(part(keep_e, y, m), part(got_e, y, m), swap(far_e, "y"))
    keep = [keep0, keep1, keep2]
    recv = [swap(give0, "c"), swap(give1, "c"), swap(give2, "c")]
    out_mine, out_other = layer_output(after(me, sum_r, sum_e, keep2), keep, recv, qb, mid)
    sum_r = halve(sum_r, y, m)
    sum_e = add(sum_e[0], swap(sum_e[1], "x"), bf16)
    feed_line = jnp.stack([wide(sum_e), sum_r], 1)
    keep_a, send_a, keep_b, send_b, grad_mine, grad_other = back(
        after(me, out_mine), keep, recv, u, t, low, qa, qb, vec, eb, sums_two, r
    )
    feed_pieces = line_pieces(feed_line, m)
    layer_out = exchange(out_mine, out_other, x)
    got_a, got_b = swap(send_a, "c"), swap(send_b, "c")
    far_a = add(keep_a[1], got_a[1], bf16)
    far_b = add(part(keep_b, 1 - y, m), part(got_b, 1 - y, m), bf16)
    line_a = halve(add3(keep_a[0], got_a[0], swap(far_a, "x")), y, m)
    sum_b = add3(part(keep_b, y, m), part(got_b, y, m), swap(far_b, "y"))
    line_b = add(sum_b[0], swap(sum_b[1], "x"), bf16)
    input_grad = exchange(grad_mine, after(grad_other, layer_out), x)
    line = jnp.concatenate([line_a, line_b], 2)
    mats, v, packed_vec, expand_vec = finish(line_pieces(line, m), feed_pieces)
    packed_grad, output_grad, expand_grad, reduce_grad = mats
    return (
        layer_out,
        input_grad,
        v[0],
        v[1],
        v[2],
        v[3],
        packed_grad,
        packed_vec,
        output_grad,
        v[4],
        expand_grad,
        expand_vec,
        reduce_grad,
        v[4],
    )


def solution(mesh):
    shard = mesh.shape["shard"]
    m = shard // 2
    fine = Mesh(mesh.devices.reshape(2, 2, m, 2), ("x", "c", "z", "y"))
    every = ("x", "c", "z", "y")
    tokens = P(("z", "y"), ("x", "c"), None)
    vec, mat = P(every), P(every, None)
    in_specs = (tokens, vec, vec, vec, vec, mat, P(None, every), mat, vec, mat, vec, mat, vec, tokens)
    out_specs = (tokens, tokens, vec, vec, vec, vec, mat, P(None, every), mat, vec, mat, vec, mat, vec)

    def body(*args):
        return shards(*args, m=m)

    return jax.shard_map(body, mesh=fine, in_specs=in_specs, out_specs=out_specs, check_vma=False)
```
